256 devices in a mesh: tm: 8 (over y, core), space: 32 (over z, x).
Axes of the slice: x: 4, y: 4, z: 8, core: 2. Of those that a mesh axis runs over, the one named last changes fastest.
Arguments:
- start_field: float32 [2048, 512], P('space'), may hold values from -6 to 6
- guessed: float32 [32, 2048, 512], P('tm', 'space'), may hold values from -6 to 6
- diffusion: float32 [2048, 512], P('space'), may hold values from 0.02 to 0.3
- peclet_x: float32 [2048, 512], P('space'), may hold values from -0.9 to 0.9
- peclet_y: float32 [2048, 512], P('space'), may hold values from -0.9 to 0.9
- source: float32 [2048, 512], P('space'), may hold values from -0.3 to 0.3
Outputs:
- corrected: float32 [32, 2048, 512], P('tm', 'space')
The draws below stay inside these ranges and needn't reach their ends.
All inputs are finite; a program needn't handle non-finite values.
Results may differ from the reference program's by a relative error of at most 0.00002.
Values sent between devices are 32-bit elements; how exact they have to be, the bound alone decides.
A program may use at most 64 MiB of HBM per device.

```python
import math
import jax
import jax.numpy as jnp

COLUMNS = 512
SUBSTEPS = 4
COARSEN_ONE = 8
COARSEN_TWO = 4
SLABS = 8
C_POINTS = 32
GRID_ROWS = 2048


def shard_levels(stream_key, extent, cuts, least, high):
    def one(dim, blocks):
        steps = jax.random.uniform(jax.random.fold_in(jax.random.fold_in(stream_key, 6), dim), (blocks,), jnp.float32, least / len(cuts), high / len(cuts))
        return jnp.repeat(jnp.exp(steps), extent[dim] // blocks).reshape((-1,) + (1,) * (len(extent) - dim - 1))

    loudness = one(*cuts[0])
    for cut in cuts[1:]:
        loudness = loudness * one(*cut)
    return loudness


def noise(own_key, shape, scale, reach, cuts=(), dtype=jnp.bfloat16):
    values = scale * jax.random.normal(own_key, shape, jnp.float32)
    if cuts:
        values = values * shard_levels(own_key, shape, cuts, -0.22, 0.18)
    return jnp.clip(values, -reach, reach).astype(dtype)


def setup_inputs(seed: int = 0) -> dict:
    arg_keys = jax.random.split(jax.random.key(seed), 7)
    return {
        "start_field": noise(arg_keys[0], (GRID_ROWS, COLUMNS), 1.0, 6.0, ((0, 32),), jnp.float32),
        "guessed": noise(arg_keys[1], (C_POINTS, GRID_ROWS, COLUMNS), 1.0, 6.0, ((0, 8), (1, 32)), jnp.float32),
        "diffusion": jnp.clip(jnp.exp(math.log(0.3) - 2.7080503 * jax.random.uniform(arg_keys[2], (GRID_ROWS, COLUMNS), jnp.float32) ** shard_levels(arg_keys[2], (GRID_ROWS, COLUMNS), ((0, 32),), -0.2, 0.2)), 0.02, 0.3),
        "peclet_x": jnp.clip(jax.random.uniform(arg_keys[3], (GRID_ROWS, COLUMNS), jnp.float32, -0.9, 0.9) * shard_levels(arg_keys[3], (GRID_ROWS, COLUMNS), ((0, 32),), -0.4, 0.0), -0.9, 0.9),
        "peclet_y": jnp.clip(jax.random.uniform(arg_keys[4], (GRID_ROWS, COLUMNS), jnp.float32, -0.9, 0.9) * shard_levels(arg_keys[4], (GRID_ROWS, COLUMNS), ((0, 32),), -0.4, 0.0), -0.9, 0.9),
        "source": noise(arg_keys[5], (GRID_ROWS, COLUMNS), 0.05, 0.3, ((0, 32),), jnp.float32),
    }


def substep(current, coeffs, step_scale, with_source):
    diffusion, peclet_x, peclet_y, source = coeffs
    widths = [(0, 0)] * (current.ndim - 2) + [(1, 1), (1, 1)]
    padded = jnp.pad(current, widths)
    north_row = padded[..., :-2, 1:-1]
    south_row = padded[..., 2:, 1:-1]
    west_col = padded[..., 1:-1, :-2]
    east_col = padded[..., 1:-1, 2:]
    inflow = diffusion * ((north_row + south_row + west_col + east_col) + peclet_x * (west_col - east_col) + peclet_y * (north_row - south_row))
    if with_source:
        inflow = inflow + source
    return (current + step_scale * inflow) / (1.0 + 4.0 * step_scale * diffusion)


def propagate(current, coeffs, step_scale, with_source):
    for position in range(SUBSTEPS):
        current = substep(current, coeffs, step_scale, with_source)
    return current


def reference(start_field, guessed, diffusion, peclet_x, peclet_y, source):
    coeffs = (diffusion, peclet_x, peclet_y, source)

    def relaxed(points):
        before = jnp.concatenate([start_field[None], points[:-1]], 0)
        for position in range(COARSEN_ONE):
            before = propagate(before, coeffs, 1.0, True)
        return before

    settled = relaxed(guessed)
    residual = relaxed(settled) - settled
    blocks = residual.reshape(SLABS, COARSEN_TWO, GRID_ROWS, COLUMNS)
    level_scale = float(COARSEN_ONE)
    top_scale = float(COARSEN_ONE * COARSEN_TWO)

    def coarse_step(current):
        return propagate(current, coeffs, level_scale, False)

    running = blocks[:, 0]
    for position in range(1, COARSEN_TWO):
        running = coarse_step(running) + blocks[:, position]
    c_value = running
    zero_block = jnp.zeros_like(c_value[:1])
    entering = jnp.concatenate([zero_block, c_value[:-1]], 0)
    running = entering
    for position in range(COARSEN_TWO - 1):
        running = coarse_step(running) + blocks[:, position]
    defect = (blocks[:, COARSEN_TWO - 1] + coarse_step(running)) - c_value
    running_value = jnp.zeros_like(defect[0])
    level_list = []
    for position in range(SLABS):
        running_value = propagate(running_value, coeffs, top_scale, False) + defect[position]
        level_list.append(running_value)
    c_fixed = c_value + jnp.stack(level_list, 0)
    running = jnp.concatenate([zero_block, c_fixed[:-1]], 0)
    pieces = []
    for position in range(COARSEN_TWO - 1):
        running = coarse_step(running) + blocks[:, position]
        pieces.append(running)
    pieces.append(c_fixed)
    fixed_all = jnp.stack(pieces, 1).reshape(C_POINTS, GRID_ROWS, COLUMNS)
    return settled + fixed_all
```

```python
import jax
import jax.numpy as jnp
from jax import lax
from jax.sharding import PartitionSpec as P

SUBSTEPS = 4
COARSEN_ONE = 8
COARSEN_TWO = 4
SWEEP = SUBSTEPS * COARSEN_ONE
COEFF_HALO = 44
RES_HALO = 3 * SUBSTEPS
LEVEL_HALO = 36


def moved(x, dt, ds):
    tms, sps = lax.axis_size("tm"), lax.axis_size("space")
    pairs = [
        (t * sps + s, (t + dt) * sps + (s + ds))
        for t in range(tms)
        for s in range(sps)
        if 0 <= t + dt < tms and 0 <= s + ds < sps
    ]
    return lax.ppermute(x, ("tm", "space"), pairs)


def with_halo(block, width, dt=0):
    rows = block.shape[-2]
    low = moved(block[..., rows - width :, :], dt, 1)
    high = moved(block[..., :width, :], dt, -1)
    middle = block if dt == 0 else moved(block, dt, 0)
    return jnp.concatenate([low, middle, high], axis=-2)


def trim(x, halo, keep):
    return x[..., halo - keep : x.shape[-2] - halo + keep, :]


def substep(extended, window, step_scale, with_source):
    middle = extended[..., 1:-1, :]
    north_row = extended[..., :-2, :]
    south_row = extended[..., 2:, :]
    widths = [(0, 0)] * (middle.ndim - 1) + [(1, 1)]
    padded = jnp.pad(middle, widths)
    west_col = padded[..., :-2]
    east_col = padded[..., 2:]
    rate_field = window[0]
    inflow = rate_field * (
        north_row
        + south_row
        + west_col
        + east_col
        + window[1] * (west_col - east_col)
        + window[2] * (north_row - south_row)
    )
    if with_source:
        inflow = inflow + window[3]
    return (middle + step_scale * inflow) / (1.0 + 4.0 * step_scale * rate_field)


def advance(fields, halo, count, coeffs, step_scale, with_source):
    inner = coeffs.shape[-2] - 2 * COEFF_HALO
    for position in range(count):
        out_halo = halo - position - 1
        first = COEFF_HALO - out_halo
        window = coeffs[:, first : first + inner + 2 * out_halo, :]
        fields = substep(fields, window, step_scale, with_source)
    return fields


def on_device(start_field, guessed, diffusion, peclet_x, peclet_y, source):
    stacked = jnp.stack([diffusion, peclet_x, peclet_y, source], 0)
    coeffs = with_halo(stacked, COEFF_HALO)
    start_ext = with_halo(start_field, COEFF_HALO)
    my_index = lax.axis_index("tm")
    first_slab = my_index == 0
    level_scale = float(COARSEN_ONE)
    top_scale = float(COARSEN_ONE * COARSEN_TWO)

    def before(points, halo):
        arriving = with_halo(points[-1], halo, dt=1)
        opening = jnp.where(first_slab, trim(start_ext, COEFF_HALO, halo), arriving)
        local = with_halo(points[:-1], halo)
        return jnp.concatenate([opening[None], local], 0)

    settled = advance(before(guessed, SWEEP), SWEEP, SWEEP, coeffs, 1.0, True)

    settled_halo = SWEEP + RES_HALO
    settled_ext = with_halo(settled, settled_halo)
    arriving = with_halo(settled[-1], settled_halo, dt=1)
    opening = jnp.where(first_slab, trim(start_ext, COEFF_HALO, settled_halo), arriving)
    before2 = jnp.concatenate([opening[None], settled_ext[:-1]], 0)
    swept = advance(before2, settled_halo, SWEEP, coeffs, 1.0, True)
    residual = swept - trim(settled_ext, settled_halo, RES_HALO)

    def coarse(x, halo):
        return advance(x, halo, SUBSTEPS, coeffs, level_scale, False)

    def r_at(position, keep):
        return trim(residual[position], RES_HALO, keep)

    running = r_at(0, RES_HALO)
    halo = RES_HALO
    for position in range(1, COARSEN_TWO):
        running = coarse(running, halo) + r_at(position, halo - SUBSTEPS)
        halo -= SUBSTEPS
    c_value = running

    entering = with_halo(c_value, 4 * SUBSTEPS, dt=1)
    running = entering
    halo = 4 * SUBSTEPS
    for position in range(COARSEN_TWO - 1):
        running = coarse(running, halo) + r_at(position, halo - SUBSTEPS)
        halo -= SUBSTEPS
    defect = (r_at(COARSEN_TWO - 1, 0) + coarse(running, halo)) - c_value

    defects = lax.all_gather(with_halo(defect, LEVEL_HALO), "tm")
    tm_count = defects.shape[0]
    level_value = jnp.zeros_like(defects[0, :, :])
    level_value = jnp.pad(level_value, ((SUBSTEPS, SUBSTEPS), (0, 0)))
    halo = LEVEL_HALO + SUBSTEPS
    kept = []
    finals = []
    for position in range(tm_count):
        level_value = advance(level_value, halo, SUBSTEPS, coeffs, top_scale, False)
        halo -= SUBSTEPS
        level_value = level_value + trim(defects[position], LEVEL_HALO, halo)
        kept.append(trim(level_value, halo, min(halo, RES_HALO)) if halo >= RES_HALO else None)
        finals.append(trim(level_value, halo, 0))
    earlier = jnp.stack([k for k in kept[: tm_count - 1]], 0)
    mine = lax.dynamic_index_in_dim(jnp.stack(finals, 0), my_index, 0, keepdims=False)
    level_before = lax.dynamic_index_in_dim(
        earlier, jnp.maximum(my_index - 1, 0), 0, keepdims=False
    )

    c_fixed = c_value + mine
    running = jnp.where(
        first_slab, 0.0, trim(entering, 4 * SUBSTEPS, RES_HALO) + level_before
    )
    halo = RES_HALO
    pieces = []
    for position in range(COARSEN_TWO - 1):
        running = coarse(running, halo) + r_at(position, halo - SUBSTEPS)
        halo -= SUBSTEPS
        pieces.append(trim(running, halo, 0))
    pieces.append(c_fixed)
    return settled + jnp.stack(pieces, 0)


def solution(mesh):
    in_specs = (
        P("space", None),
        P("tm", "space", None),
        P("space", None),
        P("space", None),
        P("space", None),
        P("space", None),
    )
    out_specs = P("tm", "space", None)
    return jax.shard_map(
        on_device, mesh=mesh, in_specs=in_specs, out_specs=out_specs, check_vma=False
    )
```

```python
import functools

import jax
import jax.numpy as jnp
import numpy as np
from jax import lax
from jax.experimental import pallas as pl
from jax.experimental.pallas import tpu as pltpu
from jax.sharding import PartitionSpec as P

MESH = pl.DeviceIdType.MESH

SUBSTEPS = 4
COARSEN_ONE = 8
COARSEN_TWO = 4
SWEEP = SUBSTEPS * COARSEN_ONE
COEFF_HALO = 48
RES_HALO = 3 * SUBSTEPS
LEVEL_HALO = 40


def _shape_of(shape, index):
    return np.broadcast_to(np.float32(0), shape)[index].shape


def _present(index, offset, size):
    if offset >= 0:
        return 1 - (index + offset) // size
    return (index + offset + size) // size


def _exchange_kernel(n_in, n_out, entries, partners, fill_outs, zero_shape, *refs):
    ins = refs[:n_in]
    outs = refs[n_in : n_in + n_out]
    zeros, send_sems, recv_sems, local_sems, fill_sems, back_sems = refs[n_in + n_out :]
    me_t, me_s = lax.axis_index("tm"), lax.axis_index("space")
    tms, sps = lax.axis_size("tm"), lax.axis_size("space")

    def inside(t, s):
        return (t >= 0) & (t < tms) & (s >= 0) & (s < sps)

    def zero_view(shape):
        lead = (0,) * (3 - len(shape))
        return zeros.at[lead + tuple(slice(0, n) for n in shape)]

    zeros[...] = jnp.zeros_like(zeros)
    barrier = pltpu.get_barrier_semaphore()
    for dt, ds in partners:
        @pl.when(inside(me_t + dt, me_s + ds))
        def _():
            pl.semaphore_signal(
                barrier, 1, device_id=(me_t + dt, me_s + ds), device_id_type=MESH
            )
    peers = 0
    for dt, ds in partners:
        peers = peers + _present(me_t, dt, tms) * _present(me_s, ds, sps)
    pl.semaphore_wait(barrier, peers)

    remote = [e for e in entries if e[4] is not None]
    sends = []
    for slot, (src, src_index, dst, dst_index, offset, dynamic) in enumerate(remote):
        dt, ds = offset
        copy = pltpu.make_async_remote_copy(
            src_ref=ins[src].at[src_index],
            dst_ref=outs[dst].at[dst_index(me_t)],
            send_sem=send_sems.at[slot],
            recv_sem=recv_sems.at[slot],
            device_id=(me_t + dt, me_s + ds),
            device_id_type=MESH,
        )
        target = inside(me_t + dt, me_s + ds)

        @pl.when(target)
        def _():
            copy.start()

        sends.append((copy, target))

    locals_ = []
    for src, src_index, dst, dst_index, offset, dynamic in entries:
        if offset is not None:
            continue
        copy = pltpu.make_async_copy(
            ins[src].at[src_index], outs[dst].at[dst_index(me_t)], local_sems.at[len(locals_)]
        )
        copy.start()
        locals_.append(copy)

    fills = []
    for dst in fill_outs:
        for k in range(outs[dst].shape[0]):
            fill = pltpu.make_async_copy(
                zero_view(outs[dst].shape[1:]), outs[dst].at[k], fill_sems.at[len(fills)]
            )

            @pl.when(k > me_t)
            def _():
                fill.start()

            fills.append((k, fill))

    for slot, (src, src_index, dst, dst_index, offset, dynamic) in enumerate(remote):
        dt, ds = offset
        sender_t, sender_s = me_t - dt, me_s - ds
        has_sender = inside(sender_t, sender_s)
        incoming = pltpu.make_async_remote_copy(
            src_ref=ins[src].at[src_index],
            dst_ref=outs[dst].at[dst_index(sender_t)],
            send_sem=send_sems.at[slot],
            recv_sem=recv_sems.at[slot],
            device_id=(sender_t, sender_s),
            device_id_type=MESH,
        )

        @pl.when(has_sender)
        def _():
            incoming.wait_recv()

        missing = jnp.logical_not(has_sender)
        if dynamic:
            missing = missing & (sender_t >= 0) & (sender_t < tms)
        fallback = pltpu.make_async_copy(
            zero_view(_shape_of(ins[src].shape, src_index)),
            outs[dst].at[dst_index(sender_t)],
            back_sems.at[slot],
        )

        @pl.when(missing)
        def _():
            fallback.start()
            fallback.wait()

    for copy in locals_:
        copy.wait()
    for k, fill in fills:
        @pl.when(k > me_t)
        def _():
            fill.wait()
    for copy, target in sends:
        @pl.when(target)
        def _():
            copy.wait_send()


def exchange(inputs, out_shapes, entries, cid, fill_outs=()):
    partners = []
    for entry in entries:
        if entry[4] is None:
            continue
        dt, ds = entry[4]
        for o in ((dt, ds), (-dt, -ds)):
            if o not in partners:
                partners.append(o)
    shapes = [_shape_of(inputs[e[0]].shape, e[1]) for e in entries]
    shapes += [tuple(out_shapes[dst][1:]) for dst in fill_outs]
    padded = [(1,) * (3 - len(s)) + tuple(s) for s in shapes]
    zero_shape = tuple(max(s[i] for s in padded) for i in range(3))
    n_remote = sum(e[4] is not None for e in entries)
    n_local = sum(e[4] is None for e in entries)
    n_fill = sum(out_shapes[dst][0] for dst in fill_outs)
    kernel = functools.partial(
        _exchange_kernel,
        len(inputs),
        len(out_shapes),
        tuple(entries),
        tuple(partners),
        tuple(fill_outs),
        zero_shape,
    )
    return pl.pallas_call(
        kernel,
        out_shape=[jax.ShapeDtypeStruct(s, jnp.float32) for s in out_shapes],
        in_specs=[pl.BlockSpec(memory_space=pltpu.VMEM)] * len(inputs),
        out_specs=[pl.BlockSpec(memory_space=pl.ANY)] * len(out_shapes),
        scratch_shapes=[
            pltpu.VMEM(zero_shape, jnp.float32),
            pltpu.SemaphoreType.DMA((max(n_remote, 1),)),
            pltpu.SemaphoreType.DMA((max(n_remote, 1),)),
            pltpu.SemaphoreType.DMA((max(n_local, 1),)),
            pltpu.SemaphoreType.DMA((max(n_fill, 1),)),
            pltpu.SemaphoreType.DMA((max(n_remote, 1),)),
        ],
        compiler_params=pltpu.CompilerParams(collective_id=cid, has_side_effects=True),
    )(*inputs)


def fixed_rows(index):
    return lambda sender: index


def moved(x, dt, ds):
    tms, sps = lax.axis_size("tm"), lax.axis_size("space")
    pairs = [
        (t * sps + s, (t + dt) * sps + (s + ds))
        for t in range(tms)
        for s in range(sps)
        if 0 <= t + dt < tms and 0 <= s + ds < sps
    ]
    return lax.ppermute(x, ("tm", "space"), pairs)


def with_halo(block, width, dt=0):
    rows = block.shape[-2]
    low = moved(block[..., rows - width :, :], dt, 1)
    high = moved(block[..., :width, :], dt, -1)
    middle = block if dt == 0 else moved(block, dt, 0)
    return jnp.concatenate([low, middle, high], axis=-2)


def trim(x, halo, keep):
    return x[..., halo - keep : x.shape[-2] - halo + keep, :]


def substep(extended, window, step_scale, with_source):
    middle = extended[..., 1:-1, :]
    north_row = extended[..., :-2, :]
    south_row = extended[..., 2:, :]
    widths = [(0, 0)] * (middle.ndim - 1) + [(1, 1)]
    padded = jnp.pad(middle, widths)
    west_col = padded[..., :-2]
    east_col = padded[..., 2:]
    rate_field = window[0]
    inflow = rate_field * (
        north_row
        + south_row
        + west_col
        + east_col
        + window[1] * (west_col - east_col)
        + window[2] * (north_row - south_row)
    )
    if with_source:
        inflow = inflow + window[3]
    return (middle + step_scale * inflow) / (1.0 + 4.0 * step_scale * rate_field)


def advance(fields, halo, count, coeffs, step_scale, with_source):
    inner = coeffs.shape[-2] - 2 * COEFF_HALO
    for position in range(count):
        out_halo = halo - position - 1
        first = COEFF_HALO - out_halo
        window = coeffs[:, first : first + inner + 2 * out_halo, :]
        fields = substep(fields, window, step_scale, with_source)
    return fields


def on_device(start_field, guessed, diffusion, peclet_x, peclet_y, source):
    rows, cols = start_field.shape
    R, H, L, h = rows, COEFF_HALO, LEVEL_HALO, SWEEP
    F = fixed_rows
    stacked = jnp.stack([diffusion, peclet_x, peclet_y, source], 0)
    first_points = [
        (0, (slice(0, 3), slice(0, R)), 0, F((slice(1, 4), slice(h, h + R))), None, False),
        (0, (slice(0, 3), slice(R - h, R)), 0, F((slice(1, 4), slice(0, h))), (0, 1), False),
        (0, (slice(0, 3), slice(0, h)), 0, F((slice(1, 4), slice(h + R, 2 * h + R))), (0, -1), False),
        (0, (3, slice(0, R)), 0, F((0, slice(h, h + R))), (1, 0), False),
        (0, (3, slice(R - h, R)), 0, F((0, slice(0, h))), (1, 1), False),
        (0, (3, slice(0, h)), 0, F((0, slice(h + R, 2 * h + R))), (1, -1), False),
        (1, (slice(0, R),), 1, F((slice(H, H + R),)), None, False),
        (1, (slice(R - H, R),), 1, F((slice(0, H),)), (0, 1), False),
        (1, (slice(0, H),), 1, F((slice(H + R, 2 * H + R),)), (0, -1), False),
        (2, (slice(0, 4), slice(0, R)), 2, F((slice(0, 4), slice(H, H + R))), None, False),
        (2, (slice(0, 4), slice(R - H, R)), 2, F((slice(0, 4), slice(0, H))), (0, 1), False),
        (2, (slice(0, 4), slice(0, H)), 2, F((slice(0, 4), slice(H + R, 2 * H + R))), (0, -1), False),
    ]
    ext1, start_ext, coeffs = exchange(
        [guessed, start_field, stacked],
        [(4, 2 * h + R, cols), (2 * H + R, cols), (4, 2 * H + R, cols)],
        first_points,
        1,
    )
    my_index = lax.axis_index("tm")
    first_slab = my_index == 0
    level_scale = float(COARSEN_ONE)
    top_scale = float(COARSEN_ONE * COARSEN_TWO)

    opening = jnp.where(first_slab, trim(start_ext, H, h), ext1[0])
    before1 = jnp.concatenate([opening[None], ext1[1:]], 0)
    settled = advance(before1, h, SWEEP, coeffs, 1.0, True)

    second_points = [
        (0, (slice(0, 4), slice(0, R)), 0, F((slice(1, 5), slice(H, H + R))), None, False),
        (0, (slice(0, 4), slice(R - H, R)), 0, F((slice(1, 5), slice(0, H))), (0, 1), False),
        (0, (slice(0, 4), slice(0, H)), 0, F((slice(1, 5), slice(H + R, 2 * H + R))), (0, -1), False),
        (0, (3, slice(0, R)), 0, F((0, slice(H, H + R))), (1, 0), False),
        (0, (3, slice(R - H, R)), 0, F((0, slice(0, H))), (1, 1), False),
        (0, (3, slice(0, H)), 0, F((0, slice(H + R, 2 * H + R))), (1, -1), False),
    ]
    (ext2,) = exchange([settled], [(5, 2 * H + R, cols)], second_points, 2)
    opening = jnp.where(first_slab, start_ext, ext2[0])
    before2 = jnp.concatenate([opening[None], ext2[1:4]], 0)
    swept = advance(before2, H, SWEEP, coeffs, 1.0, True)
    residual = swept - trim(ext2[1:5], H, H - SWEEP)
    stored = H - SWEEP

    def coarse(x, halo):
        return advance(x, halo, SUBSTEPS, coeffs, level_scale, False)

    def r_at(position, keep):
        return trim(residual[position], stored, keep)

    running = r_at(0, RES_HALO)
    halo = RES_HALO
    for position in range(1, COARSEN_TWO):
        running = coarse(running, halo) + r_at(position, halo - SUBSTEPS)
        halo -= SUBSTEPS
    c_value = running

    e = 4 * SUBSTEPS
    shift_points = [
        (0, (slice(0, R),), 0, F((slice(e, e + R),)), (1, 0), False),
        (0, (slice(R - e, R),), 0, F((slice(0, e),)), (1, 1), False),
        (0, (slice(0, e),), 0, F((slice(e + R, 2 * e + R),)), (1, -1), False),
    ]
    (entering,) = exchange([c_value], [(2 * e + R, cols)], shift_points, 3)
    running = entering
    halo = e
    for position in range(COARSEN_TWO - 1):
        running = coarse(running, halo) + r_at(position, halo - SUBSTEPS)
        halo -= SUBSTEPS
    defect = (r_at(COARSEN_TWO - 1, 0) + coarse(running, halo)) - c_value

    def at_sender(rows_there):
        return lambda sender: (sender, rows_there)

    gather_points = [
        (0, (slice(0, R),), 0, at_sender(slice(L, L + R)), None, True),
        (0, (slice(R - L, R),), 0, at_sender(slice(0, L)), (0, 1), True),
        (0, (slice(0, L),), 0, at_sender(slice(L + R, 2 * L + R)), (0, -1), True),
    ]
    tm_count = lax.axis_size("tm")
    for dt in range(1, tm_count):
        gather_points += [
            (0, (slice(0, R),), 0, at_sender(slice(L, L + R)), (dt, 0), True),
            (0, (slice(R - L, R),), 0, at_sender(slice(0, L)), (dt, 1), True),
            (0, (slice(0, L),), 0, at_sender(slice(L + R, 2 * L + R)), (dt, -1), True),
        ]
    (defects,) = exchange([defect], [(tm_count, 2 * L + R, cols)], gather_points, 4, fill_outs=(0,))

    level_value = jnp.zeros_like(defects[0, :, :])
    level_value = jnp.pad(level_value, ((SUBSTEPS, SUBSTEPS), (0, 0)))
    halo = L + SUBSTEPS
    kept = []
    finals = []
    for position in range(tm_count):
        level_value = advance(level_value, halo, SUBSTEPS, coeffs, top_scale, False)
        halo -= SUBSTEPS
        level_value = level_value + trim(defects[position], L, halo)
        kept.append(trim(level_value, halo, RES_HALO) if halo >= RES_HALO else None)
        finals.append(trim(level_value, halo, 0))
    earlier = jnp.stack([k for k in kept[: tm_count - 1]], 0)
    mine = lax.dynamic_index_in_dim(jnp.stack(finals, 0), my_index, 0, keepdims=False)
    level_before = lax.dynamic_index_in_dim(
        earlier, jnp.maximum(my_index - 1, 0), 0, keepdims=False
    )

    c_fixed = c_value + mine
    running = jnp.where(first_slab, 0.0, trim(entering, e, RES_HALO) + level_before)
    halo = RES_HALO
    pieces = []
    for position in range(COARSEN_TWO - 1):
        running = coarse(running, halo) + r_at(position, halo - SUBSTEPS)
        halo -= SUBSTEPS
        pieces.append(trim(running, halo, 0))
    pieces.append(c_fixed)
    return settled + jnp.stack(pieces, 0)


def solution(mesh):
    in_specs = (
        P("space", None),
        P("tm", "space", None),
        P("space", None),
        P("space", None),
        P("space", None),
        P("space", None),
    )
    out_specs = P("tm", "space", None)
    return jax.shard_map(
        on_device, mesh=mesh, in_specs=in_specs, out_specs=out_specs, check_vma=False
    )
```

```python
import functools

import jax
import jax.numpy as jnp
import numpy as np
from jax import lax
from jax.experimental import pallas as pl
from jax.experimental.pallas import tpu as pltpu
from jax.sharding import PartitionSpec as P

MESH = pl.DeviceIdType.MESH

SUBSTEPS = 4
COARSEN_ONE = 8
COARSEN_TWO = 4
SWEEP = SUBSTEPS * COARSEN_ONE
COEFF_HALO = 48
RES_HALO = 3 * SUBSTEPS
LEVEL_HALO = 40


def _shape_of(shape, index):
    return np.broadcast_to(np.float32(0), shape)[index].shape


def _present(index, offset, size):
    if offset >= 0:
        return 1 - (index + offset) // size
    return (index + offset + size) // size


def _exchange_kernel(n_in, n_out, entries, partners, fill_outs, zero_shape, *refs):
    ins = refs[:n_in]
    outs = refs[n_in : n_in + n_out]
    zeros, send_sems, recv_sems, local_sems, fill_sems, back_sems = refs[n_in + n_out :]
    me_t, me_s = lax.axis_index("tm"), lax.axis_index("space")
    tms, sps = lax.axis_size("tm"), lax.axis_size("space")

    def inside(t, s):
        return (t >= 0) & (t < tms) & (s >= 0) & (s < sps)

    def zero_view(shape):
        lead = (0,) * (3 - len(shape))
        return zeros.at[lead + tuple(slice(0, n) for n in shape)]

    zeros[...] = jnp.zeros_like(zeros)
    barrier = pltpu.get_barrier_semaphore()
    for dt, ds in partners:
        @pl.when(inside(me_t + dt, me_s + ds))
        def _():
            pl.semaphore_signal(
                barrier, 1, device_id=(me_t + dt, me_s + ds), device_id_type=MESH
            )
    peers = 0
    for dt, ds in partners:
        peers = peers + _present(me_t, dt, tms) * _present(me_s, ds, sps)
    pl.semaphore_wait(barrier, peers)

    remote = [e for e in entries if e[4] is not None]
    sends = []
    for slot, (src, src_index, dst, dst_index, offset, dynamic) in enumerate(remote):
        dt, ds = offset
        copy = pltpu.make_async_remote_copy(
            src_ref=ins[src].at[src_index],
            dst_ref=outs[dst].at[dst_index(me_t)],
            send_sem=send_sems.at[slot],
            recv_sem=recv_sems.at[slot],
            device_id=(me_t + dt, me_s + ds),
            device_id_type=MESH,
        )
        target = inside(me_t + dt, me_s + ds)

        @pl.when(target)
        def _():
            copy.start()

        sends.append((copy, target))

    locals_ = []
    for src, src_index, dst, dst_index, offset, dynamic in entries:
        if offset is not None:
            continue
        copy = pltpu.make_async_copy(
            ins[src].at[src_index], outs[dst].at[dst_index(me_t)], local_sems.at[len(locals_)]
        )
        copy.start()
        locals_.append(copy)

    fills = []
    for dst in fill_outs:
        for k in range(outs[dst].shape[0]):
            fill = pltpu.make_async_copy(
                zero_view(outs[dst].shape[1:]), outs[dst].at[k], fill_sems.at[len(fills)]
            )

            @pl.when(k > me_t)
            def _():
                fill.start()

            fills.append((k, fill))

    for slot, (src, src_index, dst, dst_index, offset, dynamic) in enumerate(remote):
        dt, ds = offset
        sender_t, sender_s = me_t - dt, me_s - ds
        has_sender = inside(sender_t, sender_s)
        incoming = pltpu.make_async_remote_copy(
            src_ref=ins[src].at[src_index],
            dst_ref=outs[dst].at[dst_index(sender_t)],
            send_sem=send_sems.at[slot],
            recv_sem=recv_sems.at[slot],
            device_id=(sender_t, sender_s),
            device_id_type=MESH,
        )

        @pl.when(has_sender)
        def _():
            incoming.wait_recv()

        missing = jnp.logical_not(has_sender)
        if dynamic:
            missing = missing & (sender_t >= 0) & (sender_t < tms)
        fallback = pltpu.make_async_copy(
            zero_view(_shape_of(ins[src].shape, src_index)),
            outs[dst].at[dst_index(sender_t)],
            back_sems.at[slot],
        )

        @pl.when(missing)
        def _():
            fallback.start()
            fallback.wait()

    for copy in locals_:
        copy.wait()
    for k, fill in fills:
        @pl.when(k > me_t)
        def _():
            fill.wait()
    for copy, target in sends:
        @pl.when(target)
        def _():
            copy.wait_send()


def exchange(inputs, out_shapes, entries, cid, fill_outs=()):
    partners = []
    for entry in entries:
        if entry[4] is None:
            continue
        dt, ds = entry[4]
        for o in ((dt, ds), (-dt, -ds)):
            if o not in partners:
                partners.append(o)
    shapes = [_shape_of(inputs[e[0]].shape, e[1]) for e in entries]
    shapes += [tuple(out_shapes[dst][1:]) for dst in fill_outs]
    padded = [(1,) * (3 - len(s)) + tuple(s) for s in shapes]
    zero_shape = tuple(max(s[i] for s in padded) for i in range(3))
    n_remote = sum(e[4] is not None for e in entries)
    n_local = sum(e[4] is None for e in entries)
    n_fill = sum(out_shapes[dst][0] for dst in fill_outs)
    kernel = functools.partial(
        _exchange_kernel,
        len(inputs),
        len(out_shapes),
        tuple(entries),
        tuple(partners),
        tuple(fill_outs),
        zero_shape,
    )
    return pl.pallas_call(
        kernel,
        out_shape=[jax.ShapeDtypeStruct(s, jnp.float32) for s in out_shapes],
        in_specs=[pl.BlockSpec(memory_space=pltpu.VMEM)] * len(inputs),
        out_specs=[pl.BlockSpec(memory_space=pl.ANY)] * len(out_shapes),
        scratch_shapes=[
            pltpu.VMEM(zero_shape, jnp.float32),
            pltpu.SemaphoreType.DMA((max(n_remote, 1),)),
            pltpu.SemaphoreType.DMA((max(n_remote, 1),)),
            pltpu.SemaphoreType.DMA((max(n_local, 1),)),
            pltpu.SemaphoreType.DMA((max(n_fill, 1),)),
            pltpu.SemaphoreType.DMA((max(n_remote, 1),)),
        ],
        compiler_params=pltpu.CompilerParams(collective_id=cid, has_side_effects=True),
    )(*inputs)


def fixed_rows(index):
    return lambda sender: index


CHUNK = 16
PAD = 8


def _sweep_kernel(count, scale, with_source, first, x_ref, c_ref, o_ref, buf):
    fields, rows, cols = x_ref.shape
    west_edge = lax.broadcasted_iota(jnp.int32, (CHUNK, cols), 1) == 0
    east_edge = lax.broadcasted_iota(jnp.int32, (CHUNK, cols), 1) == cols - 1
    buf[:, 0:PAD, :] = jnp.zeros((2, PAD, cols), jnp.float32)
    buf[:, PAD + rows : 2 * PAD + rows, :] = jnp.zeros((2, PAD, cols), jnp.float32)

    def one(src, dst):
        for c0 in range(0, rows, CHUNK):
            centre = buf[src, pl.ds(PAD + c0, CHUNK), :]
            north_row = buf[src, pl.ds(PAD + c0 - 1, CHUNK), :]
            south_row = buf[src, pl.ds(PAD + c0 + 1, CHUNK), :]
            west_col = jnp.where(west_edge, 0.0, pltpu.roll(centre, 1, 1))
            east_col = jnp.where(east_edge, 0.0, pltpu.roll(centre, cols - 1, 1))
            rate_field = c_ref[0, pl.ds(first + c0, CHUNK), :]
            inflow = rate_field * (
                north_row
                + south_row
                + west_col
                + east_col
                + c_ref[1, pl.ds(first + c0, CHUNK), :] * (west_col - east_col)
                + c_ref[2, pl.ds(first + c0, CHUNK), :] * (north_row - south_row)
            )
            if with_source:
                inflow = inflow + c_ref[3, pl.ds(first + c0, CHUNK), :]
            buf[dst, pl.ds(PAD + c0, CHUNK), :] = (centre + scale * inflow) / (
                1.0 + 4.0 * scale * rate_field
            )

    def two(step, carry):
        one(0, 1)
        one(1, 0)
        return carry

    for f in range(fields):
        buf[0, PAD : PAD + rows, :] = x_ref[f]
        lax.fori_loop(0, count // 2, two, 0)
        o_ref[f] = buf[0, pl.ds(PAD + count, rows - 2 * count), :]


def sweep(fields, halo, count, coeffs, step_scale, with_source):
    n, rows, cols = fields.shape
    kernel = functools.partial(
        _sweep_kernel, count, step_scale, with_source, COEFF_HALO - halo
    )
    return pl.pallas_call(
        kernel,
        out_shape=jax.ShapeDtypeStruct((n, rows - 2 * count, cols), jnp.float32),
        in_specs=[pl.BlockSpec(memory_space=pltpu.VMEM)] * 2,
        out_specs=pl.BlockSpec(memory_space=pltpu.VMEM),
        scratch_shapes=[pltpu.VMEM((2, rows + 2 * PAD, cols), jnp.float32)],
        cost_estimate=pl.CostEstimate(
            flops=25 * n * rows * cols * count, transcendentals=0, bytes_accessed=4 * (n + 4) * rows * cols
        ),
    )(fields, coeffs)


def moved(x, dt, ds):
    tms, sps = lax.axis_size("tm"), lax.axis_size("space")
    pairs = [
        (t * sps + s, (t + dt) * sps + (s + ds))
        for t in range(tms)
        for s in range(sps)
        if 0 <= t + dt < tms and 0 <= s + ds < sps
    ]
    return lax.ppermute(x, ("tm", "space"), pairs)


def with_halo(block, width, dt=0):
    rows = block.shape[-2]
    low = moved(block[..., rows - width :, :], dt, 1)
    high = moved(block[..., :width, :], dt, -1)
    middle = block if dt == 0 else moved(block, dt, 0)
    return jnp.concatenate([low, middle, high], axis=-2)


def trim(x, halo, keep):
    return x[..., halo - keep : x.shape[-2] - halo + keep, :]


def substep(extended, window, step_scale, with_source):
    middle = extended[..., 1:-1, :]
    north_row = extended[..., :-2, :]
    south_row = extended[..., 2:, :]
    widths = [(0, 0)] * (middle.ndim - 1) + [(1, 1)]
    padded = jnp.pad(middle, widths)
    west_col = padded[..., :-2]
    east_col = padded[..., 2:]
    rate_field = window[0]
    inflow = rate_field * (
        north_row
        + south_row
        + west_col
        + east_col
        + window[1] * (west_col - east_col)
        + window[2] * (north_row - south_row)
    )
    if with_source:
        inflow = inflow + window[3]
    return (middle + step_scale * inflow) / (1.0 + 4.0 * step_scale * rate_field)


def advance(fields, halo, count, coeffs, step_scale, with_source):
    inner = coeffs.shape[-2] - 2 * COEFF_HALO
    for position in range(count):
        out_halo = halo - position - 1
        first = COEFF_HALO - out_halo
        window = coeffs[:, first : first + inner + 2 * out_halo, :]
        fields = substep(fields, window, step_scale, with_source)
    return fields


def on_device(start_field, guessed, diffusion, peclet_x, peclet_y, source):
    rows, cols = start_field.shape
    R, H, L, h = rows, COEFF_HALO, LEVEL_HALO, SWEEP
    F = fixed_rows
    stacked = jnp.stack([diffusion, peclet_x, peclet_y, source], 0)
    first_points = [
        (0, (slice(0, 3), slice(0, R)), 0, F((slice(1, 4), slice(h, h + R))), None, False),
        (0, (slice(0, 3), slice(R - h, R)), 0, F((slice(1, 4), slice(0, h))), (0, 1), False),
        (0, (slice(0, 3), slice(0, h)), 0, F((slice(1, 4), slice(h + R, 2 * h + R))), (0, -1), False),
        (0, (3, slice(0, R)), 0, F((0, slice(h, h + R))), (1, 0), False),
        (0, (3, slice(R - h, R)), 0, F((0, slice(0, h))), (1, 1), False),
        (0, (3, slice(0, h)), 0, F((0, slice(h + R, 2 * h + R))), (1, -1), False),
        (1, (slice(0, R),), 1, F((slice(H, H + R),)), None, False),
        (1, (slice(R - H, R),), 1, F((slice(0, H),)), (0, 1), False),
        (1, (slice(0, H),), 1, F((slice(H + R, 2 * H + R),)), (0, -1), False),
        (2, (slice(0, 4), slice(0, R)), 2, F((slice(0, 4), slice(H, H + R))), None, False),
        (2, (slice(0, 4), slice(R - H, R)), 2, F((slice(0, 4), slice(0, H))), (0, 1), False),
        (2, (slice(0, 4), slice(0, H)), 2, F((slice(0, 4), slice(H + R, 2 * H + R))), (0, -1), False),
    ]
    ext1, start_ext, coeffs = exchange(
        [guessed, start_field, stacked],
        [(4, 2 * h + R, cols), (2 * H + R, cols), (4, 2 * H + R, cols)],
        first_points,
        1,
    )
    my_index = lax.axis_index("tm")
    first_slab = my_index == 0
    level_scale = float(COARSEN_ONE)
    top_scale = float(COARSEN_ONE * COARSEN_TWO)

    opening = jnp.where(first_slab, trim(start_ext, H, h), ext1[0])
    before1 = jnp.concatenate([opening[None], ext1[1:]], 0)
    settled = sweep(before1, h, SWEEP, coeffs, 1.0, True)

    second_points = [
        (0, (slice(0, 4), slice(0, R)), 0, F((slice(1, 5), slice(H, H + R))), None, False),
        (0, (slice(0, 4), slice(R - H, R)), 0, F((slice(1, 5), slice(0, H))), (0, 1), False),
        (0, (slice(0, 4), slice(0, H)), 0, F((slice(1, 5), slice(H + R, 2 * H + R))), (0, -1), False),
        (0, (3, slice(0, R)), 0, F((0, slice(H, H + R))), (1, 0), False),
        (0, (3, slice(R - H, R)), 0, F((0, slice(0, H))), (1, 1), False),
        (0, (3, slice(0, H)), 0, F((0, slice(H + R, 2 * H + R))), (1, -1), False),
    ]
    (ext2,) = exchange([settled], [(5, 2 * H + R, cols)], second_points, 2)
    opening = jnp.where(first_slab, start_ext, ext2[0])
    before2 = jnp.concatenate([opening[None], ext2[1:4]], 0)
    swept = sweep(before2, H, SWEEP, coeffs, 1.0, True)
    residual = swept - trim(ext2[1:5], H, H - SWEEP)
    stored = H - SWEEP

    def coarse(x, halo):
        return advance(x, halo, SUBSTEPS, coeffs, level_scale, False)

    def r_at(position, keep):
        return trim(residual[position], stored, keep)

    running = r_at(0, RES_HALO)
    halo = RES_HALO
    for position in range(1, COARSEN_TWO):
        running = coarse(running, halo) + r_at(position, halo - SUBSTEPS)
        halo -= SUBSTEPS
    c_value = running

    e = 4 * SUBSTEPS
    shift_points = [
        (0, (slice(0, R),), 0, F((slice(e, e + R),)), (1, 0), False),
        (0, (slice(R - e, R),), 0, F((slice(0, e),)), (1, 1), False),
        (0, (slice(0, e),), 0, F((slice(e + R, 2 * e + R),)), (1, -1), False),
    ]
    (entering,) = exchange([c_value], [(2 * e + R, cols)], shift_points, 3)
    running = entering
    halo = e
    for position in range(COARSEN_TWO - 1):
        running = coarse(running, halo) + r_at(position, halo - SUBSTEPS)
        halo -= SUBSTEPS
    defect = (r_at(COARSEN_TWO - 1, 0) + coarse(running, halo)) - c_value

    def at_sender(rows_there):
        return lambda sender: (sender, rows_there)

    gather_points = [
        (0, (slice(0, R),), 0, at_sender(slice(L, L + R)), None, True),
        (0, (slice(R - L, R),), 0, at_sender(slice(0, L)), (0, 1), True),
        (0, (slice(0, L),), 0, at_sender(slice(L + R, 2 * L + R)), (0, -1), True),
    ]
    tm_count = lax.axis_size("tm")
    for dt in range(1, tm_count):
        gather_points += [
            (0, (slice(0, R),), 0, at_sender(slice(L, L + R)), (dt, 0), True),
            (0, (slice(R - L, R),), 0, at_sender(slice(0, L)), (dt, 1), True),
            (0, (slice(0, L),), 0, at_sender(slice(L + R, 2 * L + R)), (dt, -1), True),
        ]
    (defects,) = exchange([defect], [(tm_count, 2 * L + R, cols)], gather_points, 4, fill_outs=(0,))

    level_value = jnp.zeros_like(defects[0, :, :])
    level_value = jnp.pad(level_value, ((SUBSTEPS, SUBSTEPS), (0, 0)))
    halo = L + SUBSTEPS
    kept = []
    finals = []
    for position in range(tm_count):
        level_value = advance(level_value, halo, SUBSTEPS, coeffs, top_scale, False)
        halo -= SUBSTEPS
        level_value = level_value + trim(defects[position], L, halo)
        kept.append(trim(level_value, halo, RES_HALO) if halo >= RES_HALO else None)
        finals.append(trim(level_value, halo, 0))
    earlier = jnp.stack([k for k in kept[: tm_count - 1]], 0)
    mine = lax.dynamic_index_in_dim(jnp.stack(finals, 0), my_index, 0, keepdims=False)
    level_before = lax.dynamic_index_in_dim(
        earlier, jnp.maximum(my_index - 1, 0), 0, keepdims=False
    )

    c_fixed = c_value + mine
    running = jnp.where(first_slab, 0.0, trim(entering, e, RES_HALO) + level_before)
    halo = RES_HALO
    pieces = []
    for position in range(COARSEN_TWO - 1):
        running = coarse(running, halo) + r_at(position, halo - SUBSTEPS)
        halo -= SUBSTEPS
        pieces.append(trim(running, halo, 0))
    pieces.append(c_fixed)
    return settled + jnp.stack(pieces, 0)


def solution(mesh):
    in_specs = (
        P("space", None),
        P("tm", "space", None),
        P("space", None),
        P("space", None),
        P("space", None),
        P("space", None),
    )
    out_specs = P("tm", "space", None)
    return jax.shard_map(
        on_device, mesh=mesh, in_specs=in_specs, out_specs=out_specs, check_vma=False
    )
```

```python
import functools

import jax
import jax.numpy as jnp
import numpy as np
from jax import lax
from jax.experimental import pallas as pl
from jax.experimental.pallas import tpu as pltpu
from jax.sharding import PartitionSpec as P

MESH = pl.DeviceIdType.MESH

SUBSTEPS = 4
COARSEN_ONE = 8
COARSEN_TWO = 4
SWEEP = SUBSTEPS * COARSEN_ONE
COEFF_HALO = 48
RES_HALO = 3 * SUBSTEPS
LEVEL_HALO = 40


def _shape_of(shape, index):
    return np.broadcast_to(np.float32(0), shape)[index].shape


def _present(index, offset, size):
    if offset >= 0:
        return 1 - (index + offset) // size
    return (index + offset + size) // size


def _exchange_kernel(n_in, n_out, entries, partners, fill_outs, zero_shape, *refs):
    ins = refs[:n_in]
    outs = refs[n_in : n_in + n_out]
    zeros, send_sems, recv_sems, local_sems, fill_sems, back_sems = refs[n_in + n_out :]
    me_t, me_s = lax.axis_index("tm"), lax.axis_index("space")
    tms, sps = lax.axis_size("tm"), lax.axis_size("space")

    def inside(t, s):
        return (t >= 0) & (t < tms) & (s >= 0) & (s < sps)

    def zero_view(shape):
        lead = (0,) * (3 - len(shape))
        return zeros.at[lead + tuple(slice(0, n) for n in shape)]

    zeros[...] = jnp.zeros_like(zeros)
    barrier = pltpu.get_barrier_semaphore()
    for dt, ds in partners:
        @pl.when(inside(me_t + dt, me_s + ds))
        def _():
            pl.semaphore_signal(
                barrier, 1, device_id=(me_t + dt, me_s + ds), device_id_type=MESH
            )
    peers = 0
    for dt, ds in partners:
        peers = peers + _present(me_t, dt, tms) * _present(me_s, ds, sps)
    pl.semaphore_wait(barrier, peers)

    remote = [e for e in entries if e[4] is not None]
    sends = []
    for slot, (src, src_index, dst, dst_index, offset, dynamic) in enumerate(remote):
        dt, ds = offset
        copy = pltpu.make_async_remote_copy(
            src_ref=ins[src].at[src_index],
            dst_ref=outs[dst].at[dst_index(me_t)],
            send_sem=send_sems.at[slot],
            recv_sem=recv_sems.at[slot],
            device_id=(me_t + dt, me_s + ds),
            device_id_type=MESH,
        )
        target = inside(me_t + dt, me_s + ds)

        @pl.when(target)
        def _():
            copy.start()

        sends.append((copy, target))

    locals_ = []
    for src, src_index, dst, dst_index, offset, dynamic in entries:
        if offset is not None:
            continue
        copy = pltpu.make_async_copy(
            ins[src].at[src_index], outs[dst].at[dst_index(me_t)], local_sems.at[len(locals_)]
        )
        copy.start()
        locals_.append(copy)

    fills = []
    for dst in fill_outs:
        for k in range(outs[dst].shape[0]):
            fill = pltpu.make_async_copy(
                zero_view(outs[dst].shape[1:]), outs[dst].at[k], fill_sems.at[len(fills)]
            )

            @pl.when(k > me_t)
            def _():
                fill.start()

            fills.append((k, fill))

    for slot, (src, src_index, dst, dst_index, offset, dynamic) in enumerate(remote):
        dt, ds = offset
        sender_t, sender_s = me_t - dt, me_s - ds
        has_sender = inside(sender_t, sender_s)
        incoming = pltpu.make_async_remote_copy(
            src_ref=ins[src].at[src_index],
            dst_ref=outs[dst].at[dst_index(sender_t)],
            send_sem=send_sems.at[slot],
            recv_sem=recv_sems.at[slot],
            device_id=(sender_t, sender_s),
            device_id_type=MESH,
        )

        @pl.when(has_sender)
        def _():
            incoming.wait_recv()

        missing = jnp.logical_not(has_sender)
        if dynamic:
            missing = missing & (sender_t >= 0) & (sender_t < tms)
        fallback = pltpu.make_async_copy(
            zero_view(_shape_of(ins[src].shape, src_index)),
            outs[dst].at[dst_index(sender_t)],
            back_sems.at[slot],
        )

        @pl.when(missing)
        def _():
            fallback.start()
            fallback.wait()

    for copy in locals_:
        copy.wait()
    for k, fill in fills:
        @pl.when(k > me_t)
        def _():
            fill.wait()
    for copy, target in sends:
        @pl.when(target)
        def _():
            copy.wait_send()


def exchange(inputs, out_shapes, entries, cid, fill_outs=()):
    partners = []
    for entry in entries:
        if entry[4] is None:
            continue
        dt, ds = entry[4]
        for o in ((dt, ds), (-dt, -ds)):
            if o not in partners:
                partners.append(o)
    shapes = [_shape_of(inputs[e[0]].shape, e[1]) for e in entries]
    shapes += [tuple(out_shapes[dst][1:]) for dst in fill_outs]
    padded = [(1,) * (3 - len(s)) + tuple(s) for s in shapes]
    zero_shape = tuple(max(s[i] for s in padded) for i in range(3))
    n_remote = sum(e[4] is not None for e in entries)
    n_local = sum(e[4] is None for e in entries)
    n_fill = sum(out_shapes[dst][0] for dst in fill_outs)
    kernel = functools.partial(
        _exchange_kernel,
        len(inputs),
        len(out_shapes),
        tuple(entries),
        tuple(partners),
        tuple(fill_outs),
        zero_shape,
    )
    return pl.pallas_call(
        kernel,
        out_shape=[jax.ShapeDtypeStruct(s, jnp.float32) for s in out_shapes],
        in_specs=[pl.BlockSpec(memory_space=pltpu.VMEM)] * len(inputs),
        out_specs=[pl.BlockSpec(memory_space=pl.ANY)] * len(out_shapes),
        scratch_shapes=[
            pltpu.VMEM(zero_shape, jnp.float32),
            pltpu.SemaphoreType.DMA((max(n_remote, 1),)),
            pltpu.SemaphoreType.DMA((max(n_remote, 1),)),
            pltpu.SemaphoreType.DMA((max(n_local, 1),)),
            pltpu.SemaphoreType.DMA((max(n_fill, 1),)),
            pltpu.SemaphoreType.DMA((max(n_remote, 1),)),
        ],
        compiler_params=pltpu.CompilerParams(collective_id=cid, has_side_effects=True),
    )(*inputs)


def fixed_rows(index):
    return lambda sender: index


CHUNK = 16
PAD = 8


def _sweep_kernel(count, with_source, first, x_ref, b_ref, o_ref, buf):
    fields, rows, cols = x_ref.shape
    buf[:, 0:PAD, :] = jnp.zeros((2, PAD, cols), jnp.float32)
    buf[:, PAD + rows : 2 * PAD + rows, :] = jnp.zeros((2, PAD, cols), jnp.float32)

    def one(src, dst):
        for c0 in range(0, rows, CHUNK):
            def weight(k):
                return b_ref[k, pl.ds(first + c0, CHUNK), :]

            centre = buf[src, pl.ds(PAD + c0, CHUNK), :]
            north_row = buf[src, pl.ds(PAD + c0 - 1, CHUNK), :]
            south_row = buf[src, pl.ds(PAD + c0 + 1, CHUNK), :]
            west_col = pltpu.roll(centre, 1, 1)
            east_col = pltpu.roll(centre, cols - 1, 1)
            new = (
                weight(0) * centre
                + weight(1) * north_row
                + weight(2) * south_row
                + weight(3) * west_col
                + weight(4) * east_col
            )
            if with_source:
                new = new + weight(5)
            buf[dst, pl.ds(PAD + c0, CHUNK), :] = new

    def two(step, carry):
        one(0, 1)
        one(1, 0)
        return carry

    for f in range(fields):
        buf[0, PAD : PAD + rows, :] = x_ref[f]
        lax.fori_loop(0, count // 2, two, 0)
        o_ref[f] = buf[0, pl.ds(PAD + count, rows - 2 * count), :]


def weights(coeffs, step_scale):
    diffusion, peclet_x, peclet_y, source = coeffs
    share = 1.0 / (1.0 + 4.0 * step_scale * diffusion)
    rate = step_scale * diffusion * share
    column = lax.broadcasted_iota(jnp.int32, diffusion.shape, diffusion.ndim - 1)
    cols = diffusion.shape[-1]
    return jnp.stack(
        [
            share,
            rate * (1.0 + peclet_y),
            rate * (1.0 - peclet_y),
            jnp.where(column == 0, 0.0, rate * (1.0 + peclet_x)),
            jnp.where(column == cols - 1, 0.0, rate * (1.0 - peclet_x)),
            step_scale * source * share,
        ],
        0,
    )


def sweep(fields, halo, count, spread, with_source):
    n, rows, cols = fields.shape
    kernel = functools.partial(_sweep_kernel, count, with_source, COEFF_HALO - halo)
    return pl.pallas_call(
        kernel,
        out_shape=jax.ShapeDtypeStruct((n, rows - 2 * count, cols), jnp.float32),
        in_specs=[pl.BlockSpec(memory_space=pltpu.VMEM)] * 2,
        out_specs=pl.BlockSpec(memory_space=pltpu.VMEM),
        scratch_shapes=[pltpu.VMEM((2, rows + 2 * PAD, cols), jnp.float32)],
        cost_estimate=pl.CostEstimate(
            flops=12 * n * rows * cols * count, transcendentals=0, bytes_accessed=4 * (n + 6) * rows * cols
        ),
    )(fields, spread)


def moved(x, dt, ds):
    tms, sps = lax.axis_size("tm"), lax.axis_size("space")
    pairs = [
        (t * sps + s, (t + dt) * sps + (s + ds))
        for t in range(tms)
        for s in range(sps)
        if 0 <= t + dt < tms and 0 <= s + ds < sps
    ]
    return lax.ppermute(x, ("tm", "space"), pairs)


def with_halo(block, width, dt=0):
    rows = block.shape[-2]
    low = moved(block[..., rows - width :, :], dt, 1)
    high = moved(block[..., :width, :], dt, -1)
    middle = block if dt == 0 else moved(block, dt, 0)
    return jnp.concatenate([low, middle, high], axis=-2)


def trim(x, halo, keep):
    return x[..., halo - keep : x.shape[-2] - halo + keep, :]


def substep(extended, window, step_scale, with_source):
    middle = extended[..., 1:-1, :]
    north_row = extended[..., :-2, :]
    south_row = extended[..., 2:, :]
    widths = [(0, 0)] * (middle.ndim - 1) + [(1, 1)]
    padded = jnp.pad(middle, widths)
    west_col = padded[..., :-2]
    east_col = padded[..., 2:]
    rate_field = window[0]
    inflow = rate_field * (
        north_row
        + south_row
        + west_col
        + east_col
        + window[1] * (west_col - east_col)
        + window[2] * (north_row - south_row)
    )
    if with_source:
        inflow = inflow + window[3]
    return (middle + step_scale * inflow) / (1.0 + 4.0 * step_scale * rate_field)


def advance(fields, halo, count, coeffs, step_scale, with_source):
    inner = coeffs.shape[-2] - 2 * COEFF_HALO
    for position in range(count):
        out_halo = halo - position - 1
        first = COEFF_HALO - out_halo
        window = coeffs[:, first : first + inner + 2 * out_halo, :]
        fields = substep(fields, window, step_scale, with_source)
    return fields


def on_device(start_field, guessed, diffusion, peclet_x, peclet_y, source):
    rows, cols = start_field.shape
    R, H, L, h = rows, COEFF_HALO, LEVEL_HALO, SWEEP
    F = fixed_rows
    stacked = jnp.stack([diffusion, peclet_x, peclet_y, source], 0)
    first_points = [
        (0, (slice(0, 3), slice(0, R)), 0, F((slice(1, 4), slice(h, h + R))), None, False),
        (0, (slice(0, 3), slice(R - h, R)), 0, F((slice(1, 4), slice(0, h))), (0, 1), False),
        (0, (slice(0, 3), slice(0, h)), 0, F((slice(1, 4), slice(h + R, 2 * h + R))), (0, -1), False),
        (0, (3, slice(0, R)), 0, F((0, slice(h, h + R))), (1, 0), False),
        (0, (3, slice(R - h, R)), 0, F((0, slice(0, h))), (1, 1), False),
        (0, (3, slice(0, h)), 0, F((0, slice(h + R, 2 * h + R))), (1, -1), False),
        (1, (slice(0, R),), 1, F((slice(H, H + R),)), None, False),
        (1, (slice(R - H, R),), 1, F((slice(0, H),)), (0, 1), False),
        (1, (slice(0, H),), 1, F((slice(H + R, 2 * H + R),)), (0, -1), False),
        (2, (slice(0, 4), slice(0, R)), 2, F((slice(0, 4), slice(H, H + R))), None, False),
        (2, (slice(0, 4), slice(R - H, R)), 2, F((slice(0, 4), slice(0, H))), (0, 1), False),
        (2, (slice(0, 4), slice(0, H)), 2, F((slice(0, 4), slice(H + R, 2 * H + R))), (0, -1), False),
    ]
    ext1, start_ext, coeffs = exchange(
        [guessed, start_field, stacked],
        [(4, 2 * h + R, cols), (2 * H + R, cols), (4, 2 * H + R, cols)],
        first_points,
        1,
    )
    my_index = lax.axis_index("tm")
    first_slab = my_index == 0
    level_scale = float(COARSEN_ONE)
    top_scale = float(COARSEN_ONE * COARSEN_TWO)

    opening = jnp.where(first_slab, trim(start_ext, H, h), ext1[0])
    before1 = jnp.concatenate([opening[None], ext1[1:]], 0)
    fine = weights(coeffs, 1.0)
    settled = sweep(before1, h, SWEEP, fine, True)

    second_points = [
        (0, (slice(0, 4), slice(0, R)), 0, F((slice(1, 5), slice(H, H + R))), None, False),
        (0, (slice(0, 4), slice(R - H, R)), 0, F((slice(1, 5), slice(0, H))), (0, 1), False),
        (0, (slice(0, 4), slice(0, H)), 0, F((slice(1, 5), slice(H + R, 2 * H + R))), (0, -1), False),
        (0, (3, slice(0, R)), 0, F((0, slice(H, H + R))), (1, 0), False),
        (0, (3, slice(R - H, R)), 0, F((0, slice(0, H))), (1, 1), False),
        (0, (3, slice(0, H)), 0, F((0, slice(H + R, 2 * H + R))), (1, -1), False),
    ]
    (ext2,) = exchange([settled], [(5, 2 * H + R, cols)], second_points, 2)
    opening = jnp.where(first_slab, start_ext, ext2[0])
    before2 = jnp.concatenate([opening[None], ext2[1:4]], 0)
    swept = sweep(before2, H, SWEEP, fine, True)
    residual = swept - trim(ext2[1:5], H, H - SWEEP)
    stored = H - SWEEP

    def coarse(x, halo):
        return advance(x, halo, SUBSTEPS, coeffs, level_scale, False)

    def r_at(position, keep):
        return trim(residual[position], stored, keep)

    running = r_at(0, RES_HALO)
    halo = RES_HALO
    for position in range(1, COARSEN_TWO):
        running = coarse(running, halo) + r_at(position, halo - SUBSTEPS)
        halo -= SUBSTEPS
    c_value = running

    e = 4 * SUBSTEPS
    shift_points = [
        (0, (slice(0, R),), 0, F((slice(e, e + R),)), (1, 0), False),
        (0, (slice(R - e, R),), 0, F((slice(0, e),)), (1, 1), False),
        (0, (slice(0, e),), 0, F((slice(e + R, 2 * e + R),)), (1, -1), False),
    ]
    (entering,) = exchange([c_value], [(2 * e + R, cols)], shift_points, 3)
    running = entering
    halo = e
    for position in range(COARSEN_TWO - 1):
        running = coarse(running, halo) + r_at(position, halo - SUBSTEPS)
        halo -= SUBSTEPS
    defect = (r_at(COARSEN_TWO - 1, 0) + coarse(running, halo)) - c_value

    def at_sender(rows_there):
        return lambda sender: (sender, rows_there)

    gather_points = [
        (0, (slice(0, R),), 0, at_sender(slice(L, L + R)), None, True),
        (0, (slice(R - L, R),), 0, at_sender(slice(0, L)), (0, 1), True),
        (0, (slice(0, L),), 0, at_sender(slice(L + R, 2 * L + R)), (0, -1), True),
    ]
    tm_count = lax.axis_size("tm")
    for dt in range(1, tm_count):
        gather_points += [
            (0, (slice(0, R),), 0, at_sender(slice(L, L + R)), (dt, 0), True),
            (0, (slice(R - L, R),), 0, at_sender(slice(0, L)), (dt, 1), True),
            (0, (slice(0, L),), 0, at_sender(slice(L + R, 2 * L + R)), (dt, -1), True),
        ]
    (defects,) = exchange([defect], [(tm_count, 2 * L + R, cols)], gather_points, 4, fill_outs=(0,))

    level_value = jnp.zeros_like(defects[0, :, :])
    level_value = jnp.pad(level_value, ((SUBSTEPS, SUBSTEPS), (0, 0)))
    halo = L + SUBSTEPS
    kept = []
    finals = []
    for position in range(tm_count):
        level_value = advance(level_value, halo, SUBSTEPS, coeffs, top_scale, False)
        halo -= SUBSTEPS
        level_value = level_value + trim(defects[position], L, halo)
        kept.append(trim(level_value, halo, RES_HALO) if halo >= RES_HALO else None)
        finals.append(trim(level_value, halo, 0))
    earlier = jnp.stack([k for k in kept[: tm_count - 1]], 0)
    mine = lax.dynamic_index_in_dim(jnp.stack(finals, 0), my_index, 0, keepdims=False)
    level_before = lax.dynamic_index_in_dim(
        earlier, jnp.maximum(my_index - 1, 0), 0, keepdims=False
    )

    c_fixed = c_value + mine
    running = jnp.where(first_slab, 0.0, trim(entering, e, RES_HALO) + level_before)
    halo = RES_HALO
    pieces = []
    for position in range(COARSEN_TWO - 1):
        running = coarse(running, halo) + r_at(position, halo - SUBSTEPS)
        halo -= SUBSTEPS
        pieces.append(trim(running, halo, 0))
    pieces.append(c_fixed)
    return settled + jnp.stack(pieces, 0)


def solution(mesh):
    in_specs = (
        P("space", None),
        P("tm", "space", None),
        P("space", None),
        P("space", None),
        P("space", None),
        P("space", None),
    )
    out_specs = P("tm", "space", None)
    return jax.shard_map(
        on_device, mesh=mesh, in_specs=in_specs, out_specs=out_specs, check_vma=False
    )
```

```python
import functools

import jax
import jax.numpy as jnp
import numpy as np
from jax import lax
from jax.experimental import pallas as pl
from jax.experimental.pallas import tpu as pltpu
from jax.sharding import PartitionSpec as P

MESH = pl.DeviceIdType.MESH

SUBSTEPS = 4
COARSEN_ONE = 8
COARSEN_TWO = 4
SWEEP = SUBSTEPS * COARSEN_ONE
COEFF_HALO = 48
RES_HALO = 3 * SUBSTEPS
LEVEL_HALO = 40


def _shape_of(shape, index):
    return np.broadcast_to(np.float32(0), shape)[index].shape


def _present(index, offset, size):
    if offset >= 0:
        return 1 - (index + offset) // size
    return (index + offset + size) // size


def _exchange_kernel(n_in, n_out, entries, partners, fill_outs, zero_shape, *refs):
    ins = refs[:n_in]
    outs = refs[n_in : n_in + n_out]
    zeros, send_sems, recv_sems, local_sems, fill_sems, back_sems = refs[n_in + n_out :]
    me_t, me_s = lax.axis_index("tm"), lax.axis_index("space")
    tms, sps = lax.axis_size("tm"), lax.axis_size("space")

    def inside(t, s):
        return (t >= 0) & (t < tms) & (s >= 0) & (s < sps)

    def zero_view(shape):
        lead = (0,) * (3 - len(shape))
        return zeros.at[lead + tuple(slice(0, n) for n in shape)]

    zeros[...] = jnp.zeros_like(zeros)
    barrier = pltpu.get_barrier_semaphore()
    for dt, ds in partners:
        @pl.when(inside(me_t + dt, me_s + ds))
        def _():
            pl.semaphore_signal(
                barrier, 1, device_id=(me_t + dt, me_s + ds), device_id_type=MESH
            )
    peers = 0
    for dt, ds in partners:
        peers = peers + _present(me_t, dt, tms) * _present(me_s, ds, sps)
    pl.semaphore_wait(barrier, peers)

    remote = [e for e in entries if e[4] is not None]
    sends = []
    for slot, (src, src_index, dst, dst_index, offset, dynamic) in enumerate(remote):
        dt, ds = offset
        copy = pltpu.make_async_remote_copy(
            src_ref=ins[src].at[src_index],
            dst_ref=outs[dst].at[dst_index(me_t)],
            send_sem=send_sems.at[slot],
            recv_sem=recv_sems.at[slot],
            device_id=(me_t + dt, me_s + ds),
            device_id_type=MESH,
        )
        target = inside(me_t + dt, me_s + ds)

        @pl.when(target)
        def _():
            copy.start()

        sends.append((copy, target))

    locals_ = []
    for src, src_index, dst, dst_index, offset, dynamic in entries:
        if offset is not None:
            continue
        copy = pltpu.make_async_copy(
            ins[src].at[src_index], outs[dst].at[dst_index(me_t)], local_sems.at[len(locals_)]
        )
        copy.start()
        locals_.append(copy)

    fills = []
    for dst in fill_outs:
        for k in range(outs[dst].shape[0]):
            fill = pltpu.make_async_copy(
                zero_view(outs[dst].shape[1:]), outs[dst].at[k], fill_sems.at[len(fills)]
            )

            @pl.when(k > me_t)
            def _():
                fill.start()

            fills.append((k, fill))

    for slot, (src, src_index, dst, dst_index, offset, dynamic) in enumerate(remote):
        dt, ds = offset
        sender_t, sender_s = me_t - dt, me_s - ds
        has_sender = inside(sender_t, sender_s)
        incoming = pltpu.make_async_remote_copy(
            src_ref=ins[src].at[src_index],
            dst_ref=outs[dst].at[dst_index(sender_t)],
            send_sem=send_sems.at[slot],
            recv_sem=recv_sems.at[slot],
            device_id=(sender_t, sender_s),
            device_id_type=MESH,
        )

        @pl.when(has_sender)
        def _():
            incoming.wait_recv()

        missing = jnp.logical_not(has_sender)
        if dynamic:
            missing = missing & (sender_t >= 0) & (sender_t < tms)
        fallback = pltpu.make_async_copy(
            zero_view(_shape_of(ins[src].shape, src_index)),
            outs[dst].at[dst_index(sender_t)],
            back_sems.at[slot],
        )

        @pl.when(missing)
        def _():
            fallback.start()
            fallback.wait()

    for copy in locals_:
        copy.wait()
    for k, fill in fills:
        @pl.when(k > me_t)
        def _():
            fill.wait()
    for copy, target in sends:
        @pl.when(target)
        def _():
            copy.wait_send()


def exchange(inputs, out_shapes, entries, cid, fill_outs=()):
    partners = []
    for entry in entries:
        if entry[4] is None:
            continue
        dt, ds = entry[4]
        for o in ((dt, ds), (-dt, -ds)):
            if o not in partners:
                partners.append(o)
    shapes = [_shape_of(inputs[e[0]].shape, e[1]) for e in entries]
    shapes += [tuple(out_shapes[dst][1:]) for dst in fill_outs]
    padded = [(1,) * (3 - len(s)) + tuple(s) for s in shapes]
    zero_shape = tuple(max(s[i] for s in padded) for i in range(3))
    n_remote = sum(e[4] is not None for e in entries)
    n_local = sum(e[4] is None for e in entries)
    n_fill = sum(out_shapes[dst][0] for dst in fill_outs)
    kernel = functools.partial(
        _exchange_kernel,
        len(inputs),
        len(out_shapes),
        tuple(entries),
        tuple(partners),
        tuple(fill_outs),
        zero_shape,
    )
    return pl.pallas_call(
        kernel,
        out_shape=[jax.ShapeDtypeStruct(s, jnp.float32) for s in out_shapes],
        in_specs=[pl.BlockSpec(memory_space=pltpu.VMEM)] * len(inputs),
        out_specs=[pl.BlockSpec(memory_space=pl.ANY)] * len(out_shapes),
        scratch_shapes=[
            pltpu.VMEM(zero_shape, jnp.float32),
            pltpu.SemaphoreType.DMA((max(n_remote, 1),)),
            pltpu.SemaphoreType.DMA((max(n_remote, 1),)),
            pltpu.SemaphoreType.DMA((max(n_local, 1),)),
            pltpu.SemaphoreType.DMA((max(n_fill, 1),)),
            pltpu.SemaphoreType.DMA((max(n_remote, 1),)),
        ],
        compiler_params=pltpu.CompilerParams(collective_id=cid, has_side_effects=True),
    )(*inputs)


def fixed_rows(index):
    return lambda sender: index


CHUNK = 16
PAD = 8


def _sweep_kernel(count, with_source, first, x_ref, b_ref, o_ref, buf):
    fields, rows, cols = x_ref.shape
    buf[:, 0:PAD, :] = jnp.zeros((2, PAD, cols), jnp.float32)
    buf[:, PAD + rows : 2 * PAD + rows, :] = jnp.zeros((2, PAD, cols), jnp.float32)

    def _chunk(c0, src, dst):
        def weight(k):
            return b_ref[k, pl.ds(first + c0, CHUNK), :]

        centre = buf[src, pl.ds(PAD + c0, CHUNK), :]
        north_row = buf[src, pl.ds(PAD + c0 - 1, CHUNK), :]
        south_row = buf[src, pl.ds(PAD + c0 + 1, CHUNK), :]
        west_col = pltpu.roll(centre, 1, 1)
        east_col = pltpu.roll(centre, cols - 1, 1)
        new = (
            weight(0) * centre
            + weight(1) * north_row
            + weight(2) * south_row
            + weight(3) * west_col
            + weight(4) * east_col
        )
        if with_source:
            new = new + weight(5)
        buf[dst, pl.ds(PAD + c0, CHUNK), :] = new

    def one(src, dst, t):
        for c0 in range(0, rows, CHUNK):
            @pl.when((c0 + CHUNK > t + 1) & (c0 < rows - t - 1))
            def _():
                _chunk(c0, src, dst)

    def two(step, carry):
        one(0, 1, 2 * step)
        one(1, 0, 2 * step + 1)
        return carry

    for f in range(fields):
        buf[0, PAD : PAD + rows, :] = x_ref[f]
        lax.fori_loop(0, count // 2, two, 0)
        o_ref[f] = buf[0, pl.ds(PAD + count, rows - 2 * count), :]


def weights(coeffs, step_scale):
    diffusion, peclet_x, peclet_y, source = coeffs
    share = 1.0 / (1.0 + 4.0 * step_scale * diffusion)
    rate = step_scale * diffusion * share
    column = lax.broadcasted_iota(jnp.int32, diffusion.shape, diffusion.ndim - 1)
    cols = diffusion.shape[-1]
    return jnp.stack(
        [
            share,
            rate * (1.0 + peclet_y),
            rate * (1.0 - peclet_y),
            jnp.where(column == 0, 0.0, rate * (1.0 + peclet_x)),
            jnp.where(column == cols - 1, 0.0, rate * (1.0 - peclet_x)),
            step_scale * source * share,
        ],
        0,
    )


def sweep(fields, halo, count, spread, with_source):
    n, rows, cols = fields.shape
    kernel = functools.partial(_sweep_kernel, count, with_source, COEFF_HALO - halo)
    return pl.pallas_call(
        kernel,
        out_shape=jax.ShapeDtypeStruct((n, rows - 2 * count, cols), jnp.float32),
        in_specs=[pl.BlockSpec(memory_space=pltpu.VMEM)] * 2,
        out_specs=pl.BlockSpec(memory_space=pltpu.VMEM),
        scratch_shapes=[pltpu.VMEM((2, rows + 2 * PAD, cols), jnp.float32)],
        cost_estimate=pl.CostEstimate(
            flops=12 * n * rows * cols * count, transcendentals=0, bytes_accessed=4 * (n + 6) * rows * cols
        ),
    )(fields, spread)


def moved(x, dt, ds):
    tms, sps = lax.axis_size("tm"), lax.axis_size("space")
    pairs = [
        (t * sps + s, (t + dt) * sps + (s + ds))
        for t in range(tms)
        for s in range(sps)
        if 0 <= t + dt < tms and 0 <= s + ds < sps
    ]
    return lax.ppermute(x, ("tm", "space"), pairs)


def with_halo(block, width, dt=0):
    rows = block.shape[-2]
    low = moved(block[..., rows - width :, :], dt, 1)
    high = moved(block[..., :width, :], dt, -1)
    middle = block if dt == 0 else moved(block, dt, 0)
    return jnp.concatenate([low, middle, high], axis=-2)


def trim(x, halo, keep):
    return x[..., halo - keep : x.shape[-2] - halo + keep, :]


def substep(extended, window, step_scale, with_source):
    middle = extended[..., 1:-1, :]
    north_row = extended[..., :-2, :]
    south_row = extended[..., 2:, :]
    widths = [(0, 0)] * (middle.ndim - 1) + [(1, 1)]
    padded = jnp.pad(middle, widths)
    west_col = padded[..., :-2]
    east_col = padded[..., 2:]
    rate_field = window[0]
    inflow = rate_field * (
        north_row
        + south_row
        + west_col
        + east_col
        + window[1] * (west_col - east_col)
        + window[2] * (north_row - south_row)
    )
    if with_source:
        inflow = inflow + window[3]
    return (middle + step_scale * inflow) / (1.0 + 4.0 * step_scale * rate_field)


def advance(fields, halo, count, coeffs, step_scale, with_source):
    inner = coeffs.shape[-2] - 2 * COEFF_HALO
    for position in range(count):
        out_halo = halo - position - 1
        first = COEFF_HALO - out_halo
        window = coeffs[:, first : first + inner + 2 * out_halo, :]
        fields = substep(fields, window, step_scale, with_source)
    return fields


def on_device(start_field, guessed, diffusion, peclet_x, peclet_y, source):
    rows, cols = start_field.shape
    R, H, L, h = rows, COEFF_HALO, LEVEL_HALO, SWEEP
    F = fixed_rows
    stacked = jnp.stack([diffusion, peclet_x, peclet_y, source], 0)
    first_points = [
        (0, (slice(0, 3), slice(0, R)), 0, F((slice(1, 4), slice(h, h + R))), None, False),
        (0, (slice(0, 3), slice(R - h, R)), 0, F((slice(1, 4), slice(0, h))), (0, 1), False),
        (0, (slice(0, 3), slice(0, h)), 0, F((slice(1, 4), slice(h + R, 2 * h + R))), (0, -1), False),
        (0, (3, slice(0, R)), 0, F((0, slice(h, h + R))), (1, 0), False),
        (0, (3, slice(R - h, R)), 0, F((0, slice(0, h))), (1, 1), False),
        (0, (3, slice(0, h)), 0, F((0, slice(h + R, 2 * h + R))), (1, -1), False),
        (1, (slice(0, R),), 1, F((slice(H, H + R),)), None, False),
        (1, (slice(R - H, R),), 1, F((slice(0, H),)), (0, 1), False),
        (1, (slice(0, H),), 1, F((slice(H + R, 2 * H + R),)), (0, -1), False),
        (2, (slice(0, 4), slice(0, R)), 2, F((slice(0, 4), slice(H, H + R))), None, False),
        (2, (slice(0, 4), slice(R - H, R)), 2, F((slice(0, 4), slice(0, H))), (0, 1), False),
        (2, (slice(0, 4), slice(0, H)), 2, F((slice(0, 4), slice(H + R, 2 * H + R))), (0, -1), False),
    ]
    ext1, start_ext, coeffs = exchange(
        [guessed, start_field, stacked],
        [(4, 2 * h + R, cols), (2 * H + R, cols), (4, 2 * H + R, cols)],
        first_points,
        1,
    )
    my_index = lax.axis_index("tm")
    first_slab = my_index == 0
    level_scale = float(COARSEN_ONE)
    top_scale = float(COARSEN_ONE * COARSEN_TWO)

    opening = jnp.where(first_slab, trim(start_ext, H, h), ext1[0])
    before1 = jnp.concatenate([opening[None], ext1[1:]], 0)
    fine = weights(coeffs, 1.0)
    settled = sweep(before1, h, SWEEP, fine, True)

    second_points = [
        (0, (slice(0, 4), slice(0, R)), 0, F((slice(1, 5), slice(H, H + R))), None, False),
        (0, (slice(0, 4), slice(R - H, R)), 0, F((slice(1, 5), slice(0, H))), (0, 1), False),
        (0, (slice(0, 4), slice(0, H)), 0, F((slice(1, 5), slice(H + R, 2 * H + R))), (0, -1), False),
        (0, (3, slice(0, R)), 0, F((0, slice(H, H + R))), (1, 0), False),
        (0, (3, slice(R - H, R)), 0, F((0, slice(0, H))), (1, 1), False),
        (0, (3, slice(0, H)), 0, F((0, slice(H + R, 2 * H + R))), (1, -1), False),
    ]
    (ext2,) = exchange([settled], [(5, 2 * H + R, cols)], second_points, 2)
    opening = jnp.where(first_slab, start_ext, ext2[0])
    before2 = jnp.concatenate([opening[None], ext2[1:4]], 0)
    swept = sweep(before2, H, SWEEP, fine, True)
    residual = swept - trim(ext2[1:5], H, H - SWEEP)
    stored = H - SWEEP

    def coarse(x, halo):
        return advance(x, halo, SUBSTEPS, coeffs, level_scale, False)

    def r_at(position, keep):
        return trim(residual[position], stored, keep)

    running = r_at(0, RES_HALO)
    halo = RES_HALO
    for position in range(1, COARSEN_TWO):
        running = coarse(running, halo) + r_at(position, halo - SUBSTEPS)
        halo -= SUBSTEPS
    c_value = running

    e = 4 * SUBSTEPS
    shift_points = [
        (0, (slice(0, R),), 0, F((slice(e, e + R),)), (1, 0), False),
        (0, (slice(R - e, R),), 0, F((slice(0, e),)), (1, 1), False),
        (0, (slice(0, e),), 0, F((slice(e + R, 2 * e + R),)), (1, -1), False),
    ]
    (entering,) = exchange([c_value], [(2 * e + R, cols)], shift_points, 3)
    running = entering
    halo = e
    for position in range(COARSEN_TWO - 1):
        running = coarse(running, halo) + r_at(position, halo - SUBSTEPS)
        halo -= SUBSTEPS
    defect = (r_at(COARSEN_TWO - 1, 0) + coarse(running, halo)) - c_value

    def at_sender(rows_there):
        return lambda sender: (sender, rows_there)

    gather_points = [
        (0, (slice(0, R),), 0, at_sender(slice(L, L + R)), None, True),
        (0, (slice(R - L, R),), 0, at_sender(slice(0, L)), (0, 1), True),
        (0, (slice(0, L),), 0, at_sender(slice(L + R, 2 * L + R)), (0, -1), True),
    ]
    tm_count = lax.axis_size("tm")
    for dt in range(1, tm_count):
        gather_points += [
            (0, (slice(0, R),), 0, at_sender(slice(L, L + R)), (dt, 0), True),
            (0, (slice(R - L, R),), 0, at_sender(slice(0, L)), (dt, 1), True),
            (0, (slice(0, L),), 0, at_sender(slice(L + R, 2 * L + R)), (dt, -1), True),
        ]
    (defects,) = exchange([defect], [(tm_count, 2 * L + R, cols)], gather_points, 4, fill_outs=(0,))

    level_value = jnp.zeros_like(defects[0, :, :])
    level_value = jnp.pad(level_value, ((SUBSTEPS, SUBSTEPS), (0, 0)))
    halo = L + SUBSTEPS
    kept = []
    finals = []
    for position in range(tm_count):
        level_value = advance(level_value, halo, SUBSTEPS, coeffs, top_scale, False)
        halo -= SUBSTEPS
        level_value = level_value + trim(defects[position], L, halo)
        kept.append(trim(level_value, halo, RES_HALO) if halo >= RES_HALO else None)
        finals.append(trim(level_value, halo, 0))
    earlier = jnp.stack([k for k in kept[: tm_count - 1]], 0)
    mine = lax.dynamic_index_in_dim(jnp.stack(finals, 0), my_index, 0, keepdims=False)
    level_before = lax.dynamic_index_in_dim(
        earlier, jnp.maximum(my_index - 1, 0), 0, keepdims=False
    )

    c_fixed = c_value + mine
    running = jnp.where(first_slab, 0.0, trim(entering, e, RES_HALO) + level_before)
    halo = RES_HALO
    pieces = []
    for position in range(COARSEN_TWO - 1):
        running = coarse(running, halo) + r_at(position, halo - SUBSTEPS)
        halo -= SUBSTEPS
        pieces.append(trim(running, halo, 0))
    pieces.append(c_fixed)
    return settled + jnp.stack(pieces, 0)


def solution(mesh):
    in_specs = (
        P("space", None),
        P("tm", "space", None),
        P("space", None),
        P("space", None),
        P("space", None),
        P("space", None),
    )
    out_specs = P("tm", "space", None)
    return jax.shard_map(
        on_device, mesh=mesh, in_specs=in_specs, out_specs=out_specs, check_vma=False
    )
```

```python
import functools

import jax
import jax.numpy as jnp
import numpy as np
from jax import lax
from jax.experimental import pallas as pl
from jax.experimental.pallas import tpu as pltpu
from jax.sharding import PartitionSpec as P

MESH = pl.DeviceIdType.MESH

SUBSTEPS = 4
COARSEN_ONE = 8
COARSEN_TWO = 4
SWEEP = SUBSTEPS * COARSEN_ONE
COEFF_HALO = 48
RES_HALO = 3 * SUBSTEPS
LEVEL_HALO = 40


def _shape_of(shape, index):
    return np.broadcast_to(np.float32(0), shape)[index].shape


def _present(index, offset, size):
    if offset >= 0:
        return 1 - (index + offset) // size
    return (index + offset + size) // size


def _exchange_kernel(n_in, n_out, entries, partners, fill_outs, zero_shape, *refs):
    ins = refs[:n_in]
    outs = refs[n_in : n_in + n_out]
    zeros, send_sems, recv_sems, local_sems, fill_sems, back_sems = refs[n_in + n_out :]
    me_t, me_s = lax.axis_index("tm"), lax.axis_index("space")
    tms, sps = lax.axis_size("tm"), lax.axis_size("space")

    def inside(t, s):
        return (t >= 0) & (t < tms) & (s >= 0) & (s < sps)

    def zero_view(shape):
        lead = (0,) * (3 - len(shape))
        return zeros.at[lead + tuple(slice(0, n) for n in shape)]

    zeros[...] = jnp.zeros_like(zeros)
    barrier = pltpu.get_barrier_semaphore()
    for dt, ds in partners:
        @pl.when(inside(me_t + dt, me_s + ds))
        def _():
            pl.semaphore_signal(
                barrier, 1, device_id=(me_t + dt, me_s + ds), device_id_type=MESH
            )
    peers = 0
    for dt, ds in partners:
        peers = peers + _present(me_t, dt, tms) * _present(me_s, ds, sps)
    pl.semaphore_wait(barrier, peers)

    remote = [e for e in entries if e[4] is not None]
    sends = []
    for slot, (src, src_index, dst, dst_index, offset, dynamic) in enumerate(remote):
        dt, ds = offset
        copy = pltpu.make_async_remote_copy(
            src_ref=ins[src].at[src_index],
            dst_ref=outs[dst].at[dst_index(me_t)],
            send_sem=send_sems.at[slot],
            recv_sem=recv_sems.at[slot],
            device_id=(me_t + dt, me_s + ds),
            device_id_type=MESH,
        )
        target = inside(me_t + dt, me_s + ds)

        @pl.when(target)
        def _():
            copy.start()

        sends.append((copy, target))

    locals_ = []
    for src, src_index, dst, dst_index, offset, dynamic in entries:
        if offset is not None:
            continue
        copy = pltpu.make_async_copy(
            ins[src].at[src_index], outs[dst].at[dst_index(me_t)], local_sems.at[len(locals_)]
        )
        copy.start()
        locals_.append(copy)

    fills = []
    for dst in fill_outs:
        for k in range(outs[dst].shape[0]):
            fill = pltpu.make_async_copy(
                zero_view(outs[dst].shape[1:]), outs[dst].at[k], fill_sems.at[len(fills)]
            )

            @pl.when(k > me_t)
            def _():
                fill.start()

            fills.append((k, fill))

    for slot, (src, src_index, dst, dst_index, offset, dynamic) in enumerate(remote):
        dt, ds = offset
        sender_t, sender_s = me_t - dt, me_s - ds
        has_sender = inside(sender_t, sender_s)
        incoming = pltpu.make_async_remote_copy(
            src_ref=ins[src].at[src_index],
            dst_ref=outs[dst].at[dst_index(sender_t)],
            send_sem=send_sems.at[slot],
            recv_sem=recv_sems.at[slot],
            device_id=(sender_t, sender_s),
            device_id_type=MESH,
        )

        @pl.when(has_sender)
        def _():
            incoming.wait_recv()

        missing = jnp.logical_not(has_sender)
        if dynamic:
            missing = missing & (sender_t >= 0) & (sender_t < tms)
        fallback = pltpu.make_async_copy(
            zero_view(_shape_of(ins[src].shape, src_index)),
            outs[dst].at[dst_index(sender_t)],
            back_sems.at[slot],
        )

        @pl.when(missing)
        def _():
            fallback.start()
            fallback.wait()

    for copy in locals_:
        copy.wait()
    for k, fill in fills:
        @pl.when(k > me_t)
        def _():
            fill.wait()
    for copy, target in sends:
        @pl.when(target)
        def _():
            copy.wait_send()


def exchange(inputs, out_shapes, entries, cid, fill_outs=()):
    partners = []
    for entry in entries:
        if entry[4] is None:
            continue
        dt, ds = entry[4]
        for o in ((dt, ds), (-dt, -ds)):
            if o not in partners:
                partners.append(o)
    shapes = [_shape_of(inputs[e[0]].shape, e[1]) for e in entries]
    shapes += [tuple(out_shapes[dst][1:]) for dst in fill_outs]
    padded = [(1,) * (3 - len(s)) + tuple(s) for s in shapes]
    zero_shape = tuple(max(s[i] for s in padded) for i in range(3))
    n_remote = sum(e[4] is not None for e in entries)
    n_local = sum(e[4] is None for e in entries)
    n_fill = sum(out_shapes[dst][0] for dst in fill_outs)
    kernel = functools.partial(
        _exchange_kernel,
        len(inputs),
        len(out_shapes),
        tuple(entries),
        tuple(partners),
        tuple(fill_outs),
        zero_shape,
    )
    return pl.pallas_call(
        kernel,
        out_shape=[jax.ShapeDtypeStruct(s, jnp.float32) for s in out_shapes],
        in_specs=[pl.BlockSpec(memory_space=pltpu.VMEM)] * len(inputs),
        out_specs=[pl.BlockSpec(memory_space=pl.ANY)] * len(out_shapes),
        scratch_shapes=[
            pltpu.VMEM(zero_shape, jnp.float32),
            pltpu.SemaphoreType.DMA((max(n_remote, 1),)),
            pltpu.SemaphoreType.DMA((max(n_remote, 1),)),
            pltpu.SemaphoreType.DMA((max(n_local, 1),)),
            pltpu.SemaphoreType.DMA((max(n_fill, 1),)),
            pltpu.SemaphoreType.DMA((max(n_remote, 1),)),
        ],
        compiler_params=pltpu.CompilerParams(collective_id=cid, has_side_effects=True),
    )(*inputs)


def fixed_rows(index):
    return lambda sender: index


CHUNK = 16
PAD = 8


def _stencil(buf, b_ref, first, rows, cols, src, dst, with_source):
    for c0 in range(0, rows, CHUNK):
        def weight(k):
            return b_ref[k, pl.ds(first + c0, CHUNK), :]

        centre = buf[src, pl.ds(PAD + c0, CHUNK), :]
        north_row = buf[src, pl.ds(PAD + c0 - 1, CHUNK), :]
        south_row = buf[src, pl.ds(PAD + c0 + 1, CHUNK), :]
        west_col = pltpu.roll(centre, 1, 1)
        east_col = pltpu.roll(centre, cols - 1, 1)
        new = (
            weight(0) * centre
            + weight(1) * north_row
            + weight(2) * south_row
            + weight(3) * west_col
            + weight(4) * east_col
        )
        if with_source:
            new = new + weight(5)
        buf[dst, pl.ds(PAD + c0, CHUNK), :] = new


def _sweep_kernel(count, with_source, first, x_ref, b_ref, o_ref, buf):
    fields, rows, cols = x_ref.shape
    buf[:, 0:PAD, :] = jnp.zeros((2, PAD, cols), jnp.float32)
    buf[:, PAD + rows : 2 * PAD + rows, :] = jnp.zeros((2, PAD, cols), jnp.float32)

    def two(step, carry):
        _stencil(buf, b_ref, first, rows, cols, 0, 1, with_source)
        _stencil(buf, b_ref, first, rows, cols, 1, 0, with_source)
        return carry

    for f in range(fields):
        buf[0, PAD : PAD + rows, :] = x_ref[f]
        lax.fori_loop(0, count // 2, two, 0)
        o_ref[f] = buf[0, pl.ds(PAD + count, rows - 2 * count), :]


def weights(coeffs, step_scale):
    diffusion, peclet_x, peclet_y, source = coeffs
    share = 1.0 / (1.0 + 4.0 * step_scale * diffusion)
    rate = step_scale * diffusion * share
    column = lax.broadcasted_iota(jnp.int32, diffusion.shape, diffusion.ndim - 1)
    cols = diffusion.shape[-1]
    return jnp.stack(
        [
            share,
            rate * (1.0 + peclet_y),
            rate * (1.0 - peclet_y),
            jnp.where(column == 0, 0.0, rate * (1.0 + peclet_x)),
            jnp.where(column == cols - 1, 0.0, rate * (1.0 - peclet_x)),
            step_scale * source * share,
        ],
        0,
    )


def sweep(fields, halo, count, spread, with_source):
    n, rows, cols = fields.shape
    kernel = functools.partial(_sweep_kernel, count, with_source, COEFF_HALO - halo)
    return pl.pallas_call(
        kernel,
        out_shape=jax.ShapeDtypeStruct((n, rows - 2 * count, cols), jnp.float32),
        in_specs=[pl.BlockSpec(memory_space=pltpu.VMEM)] * 2,
        out_specs=pl.BlockSpec(memory_space=pltpu.VMEM),
        scratch_shapes=[pltpu.VMEM((2, rows + 2 * PAD, cols), jnp.float32)],
        cost_estimate=pl.CostEstimate(
            flops=12 * n * rows * cols * count, transcendentals=0, bytes_accessed=4 * (n + 6) * rows * cols
        ),
    )(fields, spread)


def _level_kernel(halo, first, defect_ref, b_ref, prev_ref, mine_ref, buf, outgoing, send_sems, recv_sems):
    rows, cols = defect_ref.shape
    span = rows + 2 * halo
    me_t, me_s = lax.axis_index("tm"), lax.axis_index("space")
    tms, sps = lax.axis_size("tm"), lax.axis_size("space")

    def inside(t, s):
        return (t >= 0) & (t < tms) & (s >= 0) & (s < sps)

    buf[:, 0:PAD, :] = jnp.zeros((2, PAD, cols), jnp.float32)
    buf[:, PAD + span : 2 * PAD + span, :] = jnp.zeros((2, PAD, cols), jnp.float32)
    routes = (
        ((halo, halo + rows), (0, rows), (1, 0)),
        ((0, halo), (rows - halo, rows), (1, 1)),
        ((halo + rows, span), (0, halo), (1, -1)),
    )
    for (a, b), _, (dt, ds) in routes:
        @pl.when(jnp.logical_not(inside(me_t - dt, me_s - ds)))
        def _():
            buf[0, PAD + a : PAD + b, :] = jnp.zeros((b - a, cols), jnp.float32)

    partners = [(dt, ds) for _, _, (dt, ds) in routes] + [(-dt, -ds) for _, _, (dt, ds) in routes]
    barrier = pltpu.get_barrier_semaphore()
    peers = 0
    for dt, ds in partners:
        @pl.when(inside(me_t + dt, me_s + ds))
        def _():
            pl.semaphore_signal(
                barrier, 1, device_id=(me_t + dt, me_s + ds), device_id_type=MESH
            )
        peers = peers + _present(me_t, dt, tms) * _present(me_s, ds, sps)
    pl.semaphore_wait(barrier, peers)

    copies = []
    for slot, ((a, b), (c, d), (dt, ds)) in enumerate(routes):
        incoming = pltpu.make_async_remote_copy(
            src_ref=outgoing.at[pl.ds(c, d - c)],
            dst_ref=buf.at[0, pl.ds(PAD + a, b - a)],
            send_sem=send_sems.at[slot],
            recv_sem=recv_sems.at[slot],
            device_id=(me_t - dt, me_s - ds),
            device_id_type=MESH,
        )

        @pl.when(inside(me_t - dt, me_s - ds))
        def _():
            incoming.wait_recv()

        copies.append(
            pltpu.make_async_remote_copy(
                src_ref=outgoing.at[pl.ds(c, d - c)],
                dst_ref=buf.at[0, pl.ds(PAD + a, b - a)],
                send_sem=send_sems.at[slot],
                recv_sem=recv_sems.at[slot],
                device_id=(me_t + dt, me_s + ds),
                device_id_type=MESH,
            )
        )

    prev_ref[...] = buf[0, PAD : PAD + span, :]
    for step in range(SUBSTEPS // 2):
        _stencil(buf, b_ref, first, span, cols, 0, 1, False)
        _stencil(buf, b_ref, first, span, cols, 1, 0, False)
    mine = buf[0, PAD + halo : PAD + halo + rows, :] + defect_ref[...]
    mine_ref[...] = mine
    outgoing[...] = mine
    for copy, (_, _, (dt, ds)) in zip(copies, routes):
        @pl.when(inside(me_t + dt, me_s + ds))
        def _():
            copy.start()
    for copy, (_, _, (dt, ds)) in zip(copies, routes):
        @pl.when(inside(me_t + dt, me_s + ds))
        def _():
            copy.wait_send()


def level_chain(defect, spread, halo, cid):
    rows, cols = defect.shape
    span = rows + 2 * halo
    kernel = functools.partial(_level_kernel, halo, COEFF_HALO - halo)
    return pl.pallas_call(
        kernel,
        out_shape=[
            jax.ShapeDtypeStruct((span, cols), jnp.float32),
            jax.ShapeDtypeStruct((rows, cols), jnp.float32),
        ],
        in_specs=[pl.BlockSpec(memory_space=pltpu.VMEM)] * 2,
        out_specs=[pl.BlockSpec(memory_space=pltpu.VMEM)] * 2,
        scratch_shapes=[
            pltpu.VMEM((2, span + 2 * PAD, cols), jnp.float32),
            pltpu.VMEM((rows, cols), jnp.float32),
            pltpu.SemaphoreType.DMA((3,)),
            pltpu.SemaphoreType.DMA((3,)),
        ],
        compiler_params=pltpu.CompilerParams(collective_id=cid, has_side_effects=True),
    )(defect, spread)


def moved(x, dt, ds):
    tms, sps = lax.axis_size("tm"), lax.axis_size("space")
    pairs = [
        (t * sps + s, (t + dt) * sps + (s + ds))
        for t in range(tms)
        for s in range(sps)
        if 0 <= t + dt < tms and 0 <= s + ds < sps
    ]
    return lax.ppermute(x, ("tm", "space"), pairs)


def with_halo(block, width, dt=0):
    rows = block.shape[-2]
    low = moved(block[..., rows - width :, :], dt, 1)
    high = moved(block[..., :width, :], dt, -1)
    middle = block if dt == 0 else moved(block, dt, 0)
    return jnp.concatenate([low, middle, high], axis=-2)


def trim(x, halo, keep):
    return x[..., halo - keep : x.shape[-2] - halo + keep, :]


def substep(extended, window, step_scale, with_source):
    middle = extended[..., 1:-1, :]
    north_row = extended[..., :-2, :]
    south_row = extended[..., 2:, :]
    widths = [(0, 0)] * (middle.ndim - 1) + [(1, 1)]
    padded = jnp.pad(middle, widths)
    west_col = padded[..., :-2]
    east_col = padded[..., 2:]
    rate_field = window[0]
    inflow = rate_field * (
        north_row
        + south_row
        + west_col
        + east_col
        + window[1] * (west_col - east_col)
        + window[2] * (north_row - south_row)
    )
    if with_source:
        inflow = inflow + window[3]
    return (middle + step_scale * inflow) / (1.0 + 4.0 * step_scale * rate_field)


def advance(fields, halo, count, coeffs, step_scale, with_source):
    inner = coeffs.shape[-2] - 2 * COEFF_HALO
    for position in range(count):
        out_halo = halo - position - 1
        first = COEFF_HALO - out_halo
        window = coeffs[:, first : first + inner + 2 * out_halo, :]
        fields = substep(fields, window, step_scale, with_source)
    return fields


def on_device(start_field, guessed, diffusion, peclet_x, peclet_y, source):
    rows, cols = start_field.shape
    R, H, L, h = rows, COEFF_HALO, LEVEL_HALO, SWEEP
    F = fixed_rows
    stacked = jnp.stack([diffusion, peclet_x, peclet_y, source], 0)
    first_points = [
        (0, (slice(0, 3), slice(0, R)), 0, F((slice(1, 4), slice(h, h + R))), None, False),
        (0, (slice(0, 3), slice(R - h, R)), 0, F((slice(1, 4), slice(0, h))), (0, 1), False),
        (0, (slice(0, 3), slice(0, h)), 0, F((slice(1, 4), slice(h + R, 2 * h + R))), (0, -1), False),
        (0, (3, slice(0, R)), 0, F((0, slice(h, h + R))), (1, 0), False),
        (0, (3, slice(R - h, R)), 0, F((0, slice(0, h))), (1, 1), False),
        (0, (3, slice(0, h)), 0, F((0, slice(h + R, 2 * h + R))), (1, -1), False),
        (1, (slice(0, R),), 1, F((slice(H, H + R),)), None, False),
        (1, (slice(R - H, R),), 1, F((slice(0, H),)), (0, 1), False),
        (1, (slice(0, H),), 1, F((slice(H + R, 2 * H + R),)), (0, -1), False),
        (2, (slice(0, 4), slice(0, R)), 2, F((slice(0, 4), slice(H, H + R))), None, False),
        (2, (slice(0, 4), slice(R - H, R)), 2, F((slice(0, 4), slice(0, H))), (0, 1), False),
        (2, (slice(0, 4), slice(0, H)), 2, F((slice(0, 4), slice(H + R, 2 * H + R))), (0, -1), False),
    ]
    ext1, start_ext, coeffs = exchange(
        [guessed, start_field, stacked],
        [(4, 2 * h + R, cols), (2 * H + R, cols), (4, 2 * H + R, cols)],
        first_points,
        1,
    )
    my_index = lax.axis_index("tm")
    first_slab = my_index == 0
    level_scale = float(COARSEN_ONE)
    top_scale = float(COARSEN_ONE * COARSEN_TWO)

    opening = jnp.where(first_slab, trim(start_ext, H, h), ext1[0])
    before1 = jnp.concatenate([opening[None], ext1[1:]], 0)
    fine = weights(coeffs, 1.0)
    settled = sweep(before1, h, SWEEP, fine, True)

    second_points = [
        (0, (slice(0, 4), slice(0, R)), 0, F((slice(1, 5), slice(H, H + R))), None, False),
        (0, (slice(0, 4), slice(R - H, R)), 0, F((slice(1, 5), slice(0, H))), (0, 1), False),
        (0, (slice(0, 4), slice(0, H)), 0, F((slice(1, 5), slice(H + R, 2 * H + R))), (0, -1), False),
        (0, (3, slice(0, R)), 0, F((0, slice(H, H + R))), (1, 0), False),
        (0, (3, slice(R - H, R)), 0, F((0, slice(0, H))), (1, 1), False),
        (0, (3, slice(0, H)), 0, F((0, slice(H + R, 2 * H + R))), (1, -1), False),
    ]
    (ext2,) = exchange([settled], [(5, 2 * H + R, cols)], second_points, 2)
    opening = jnp.where(first_slab, start_ext, ext2[0])
    before2 = jnp.concatenate([opening[None], ext2[1:4]], 0)
    swept = sweep(before2, H, SWEEP, fine, True)
    residual = swept - trim(ext2[1:5], H, H - SWEEP)
    stored = H - SWEEP

    def coarse(x, halo):
        return advance(x, halo, SUBSTEPS, coeffs, level_scale, False)

    def r_at(position, keep):
        return trim(residual[position], stored, keep)

    running = r_at(0, RES_HALO)
    halo = RES_HALO
    for position in range(1, COARSEN_TWO):
        running = coarse(running, halo) + r_at(position, halo - SUBSTEPS)
        halo -= SUBSTEPS
    c_value = running

    e = 4 * SUBSTEPS
    shift_points = [
        (0, (slice(0, R),), 0, F((slice(e, e + R),)), (1, 0), False),
        (0, (slice(R - e, R),), 0, F((slice(0, e),)), (1, 1), False),
        (0, (slice(0, e),), 0, F((slice(e + R, 2 * e + R),)), (1, -1), False),
    ]
    (entering,) = exchange([c_value], [(2 * e + R, cols)], shift_points, 3)
    running = entering
    halo = e
    for position in range(COARSEN_TWO - 1):
        running = coarse(running, halo) + r_at(position, halo - SUBSTEPS)
        halo -= SUBSTEPS
    defect = (r_at(COARSEN_TWO - 1, 0) + coarse(running, halo)) - c_value

    level_halo = 16
    prev_level, mine = level_chain(defect, weights(coeffs, top_scale), level_halo, 4)
    level_before = trim(prev_level, level_halo, RES_HALO)

    c_fixed = c_value + mine
    running = jnp.where(first_slab, 0.0, trim(entering, e, RES_HALO) + level_before)
    halo = RES_HALO
    pieces = []
    for position in range(COARSEN_TWO - 1):
        running = coarse(running, halo) + r_at(position, halo - SUBSTEPS)
        halo -= SUBSTEPS
        pieces.append(trim(running, halo, 0))
    pieces.append(c_fixed)
    return settled + jnp.stack(pieces, 0)


def solution(mesh):
    in_specs = (
        P("space", None),
        P("tm", "space", None),
        P("space", None),
        P("space", None),
        P("space", None),
        P("space", None),
    )
    out_specs = P("tm", "space", None)
    return jax.shard_map(
        on_device, mesh=mesh, in_specs=in_specs, out_specs=out_specs, check_vma=False
    )
```

```python
import functools

import jax
import jax.numpy as jnp
import numpy as np
from jax import lax
from jax.experimental import pallas as pl
from jax.experimental.pallas import tpu as pltpu
from jax.sharding import PartitionSpec as P

MESH = pl.DeviceIdType.MESH

SUBSTEPS = 4
COARSEN_ONE = 8
COARSEN_TWO = 4
SWEEP = SUBSTEPS * COARSEN_ONE
COEFF_HALO = 48
RES_HALO = 3 * SUBSTEPS
LEVEL_HALO = 40


def _shape_of(shape, index):
    return np.broadcast_to(np.float32(0), shape)[index].shape


def _present(index, offset, size):
    if offset >= 0:
        return 1 - (index + offset) // size
    return (index + offset + size) // size


def _exchange_kernel(n_in, n_out, entries, partners, fill_outs, zero_shape, *refs):
    ins = refs[:n_in]
    outs = refs[n_in : n_in + n_out]
    zeros, send_sems, recv_sems, local_sems, fill_sems, back_sems = refs[n_in + n_out :]
    me_t, me_s = lax.axis_index("tm"), lax.axis_index("space")
    tms, sps = lax.axis_size("tm"), lax.axis_size("space")

    def inside(t, s):
        return (t >= 0) & (t < tms) & (s >= 0) & (s < sps)

    def zero_view(shape):
        lead = (0,) * (3 - len(shape))
        return zeros.at[lead + tuple(slice(0, n) for n in shape)]

    zeros[...] = jnp.zeros_like(zeros)
    barrier = pltpu.get_barrier_semaphore()
    for dt, ds in partners:
        @pl.when(inside(me_t + dt, me_s + ds))
        def _():
            pl.semaphore_signal(
                barrier, 1, device_id=(me_t + dt, me_s + ds), device_id_type=MESH
            )
    peers = 0
    for dt, ds in partners:
        peers = peers + _present(me_t, dt, tms) * _present(me_s, ds, sps)
    pl.semaphore_wait(barrier, peers)

    remote = [e for e in entries if e[4] is not None]
    sends = []
    for slot, (src, src_index, dst, dst_index, offset, dynamic) in enumerate(remote):
        dt, ds = offset
        copy = pltpu.make_async_remote_copy(
            src_ref=ins[src].at[src_index],
            dst_ref=outs[dst].at[dst_index(me_t)],
            send_sem=send_sems.at[slot],
            recv_sem=recv_sems.at[slot],
            device_id=(me_t + dt, me_s + ds),
            device_id_type=MESH,
        )
        target = inside(me_t + dt, me_s + ds)

        @pl.when(target)
        def _():
            copy.start()

        sends.append((copy, target))

    locals_ = []
    for src, src_index, dst, dst_index, offset, dynamic in entries:
        if offset is not None:
            continue
        copy = pltpu.make_async_copy(
            ins[src].at[src_index], outs[dst].at[dst_index(me_t)], local_sems.at[len(locals_)]
        )
        copy.start()
        locals_.append(copy)

    fills = []
    for dst in fill_outs:
        for k in range(outs[dst].shape[0]):
            fill = pltpu.make_async_copy(
                zero_view(outs[dst].shape[1:]), outs[dst].at[k], fill_sems.at[len(fills)]
            )

            @pl.when(k > me_t)
            def _():
                fill.start()

            fills.append((k, fill))

    for slot, (src, src_index, dst, dst_index, offset, dynamic) in enumerate(remote):
        dt, ds = offset
        sender_t, sender_s = me_t - dt, me_s - ds
        has_sender = inside(sender_t, sender_s)
        incoming = pltpu.make_async_remote_copy(
            src_ref=ins[src].at[src_index],
            dst_ref=outs[dst].at[dst_index(sender_t)],
            send_sem=send_sems.at[slot],
            recv_sem=recv_sems.at[slot],
            device_id=(sender_t, sender_s),
            device_id_type=MESH,
        )

        @pl.when(has_sender)
        def _():
            incoming.wait_recv()

        missing = jnp.logical_not(has_sender)
        if dynamic:
            missing = missing & (sender_t >= 0) & (sender_t < tms)
        fallback = pltpu.make_async_copy(
            zero_view(_shape_of(ins[src].shape, src_index)),
            outs[dst].at[dst_index(sender_t)],
            back_sems.at[slot],
        )

        @pl.when(missing)
        def _():
            fallback.start()
            fallback.wait()

    for copy in locals_:
        copy.wait()
    for k, fill in fills:
        @pl.when(k > me_t)
        def _():
            fill.wait()
    for copy, target in sends:
        @pl.when(target)
        def _():
            copy.wait_send()


def exchange(inputs, out_shapes, entries, cid, fill_outs=()):
    partners = []
    for entry in entries:
        if entry[4] is None:
            continue
        dt, ds = entry[4]
        for o in ((dt, ds), (-dt, -ds)):
            if o not in partners:
                partners.append(o)
    shapes = [_shape_of(inputs[e[0]].shape, e[1]) for e in entries]
    shapes += [tuple(out_shapes[dst][1:]) for dst in fill_outs]
    padded = [(1,) * (3 - len(s)) + tuple(s) for s in shapes]
    zero_shape = tuple(max(s[i] for s in padded) for i in range(3))
    n_remote = sum(e[4] is not None for e in entries)
    n_local = sum(e[4] is None for e in entries)
    n_fill = sum(out_shapes[dst][0] for dst in fill_outs)
    kernel = functools.partial(
        _exchange_kernel,
        len(inputs),
        len(out_shapes),
        tuple(entries),
        tuple(partners),
        tuple(fill_outs),
        zero_shape,
    )
    return pl.pallas_call(
        kernel,
        out_shape=[jax.ShapeDtypeStruct(s, jnp.float32) for s in out_shapes],
        in_specs=[pl.BlockSpec(memory_space=pltpu.VMEM)] * len(inputs),
        out_specs=[pl.BlockSpec(memory_space=pl.ANY)] * len(out_shapes),
        scratch_shapes=[
            pltpu.VMEM(zero_shape, jnp.float32),
            pltpu.SemaphoreType.DMA((max(n_remote, 1),)),
            pltpu.SemaphoreType.DMA((max(n_remote, 1),)),
            pltpu.SemaphoreType.DMA((max(n_local, 1),)),
            pltpu.SemaphoreType.DMA((max(n_fill, 1),)),
            pltpu.SemaphoreType.DMA((max(n_remote, 1),)),
        ],
        compiler_params=pltpu.CompilerParams(collective_id=cid, has_side_effects=True),
    )(*inputs)


def fixed_rows(index):
    return lambda sender: index


CHUNK = 16
PAD = 8


def _stencil(buf, b_ref, first, rows, cols, src, dst, with_source):
    for c0 in range(0, rows, CHUNK):
        def weight(k):
            return b_ref[k, pl.ds(first + c0, CHUNK), :]

        centre = buf[src, pl.ds(PAD + c0, CHUNK), :]
        north_row = buf[src, pl.ds(PAD + c0 - 1, CHUNK), :]
        south_row = buf[src, pl.ds(PAD + c0 + 1, CHUNK), :]
        west_col = pltpu.roll(centre, 1, 1)
        east_col = pltpu.roll(centre, cols - 1, 1)
        new = (
            weight(0) * centre
            + weight(1) * north_row
            + weight(2) * south_row
            + weight(3) * west_col
            + weight(4) * east_col
        )
        if with_source:
            new = new + weight(5)
        buf[dst, pl.ds(PAD + c0, CHUNK), :] = new


def _sweep_kernel(count, with_source, first, x_ref, b_ref, o_ref, buf):
    fields, rows, cols = x_ref.shape
    buf[:, 0:PAD, :] = jnp.zeros((2, PAD, cols), jnp.float32)
    buf[:, PAD + rows : 2 * PAD + rows, :] = jnp.zeros((2, PAD, cols), jnp.float32)

    def two(step, carry):
        _stencil(buf, b_ref, first, rows, cols, 0, 1, with_source)
        _stencil(buf, b_ref, first, rows, cols, 1, 0, with_source)
        return carry

    for f in range(fields):
        buf[0, PAD : PAD + rows, :] = x_ref[f]
        lax.fori_loop(0, count // 2, two, 0, unroll=2)
        o_ref[f] = buf[0, pl.ds(PAD + count, rows - 2 * count), :]


def weights(coeffs, step_scale):
    diffusion, peclet_x, peclet_y, source = coeffs
    share = 1.0 / (1.0 + 4.0 * step_scale * diffusion)
    rate = step_scale * diffusion * share
    column = lax.broadcasted_iota(jnp.int32, diffusion.shape, diffusion.ndim - 1)
    cols = diffusion.shape[-1]
    return jnp.stack(
        [
            share,
            rate * (1.0 + peclet_y),
            rate * (1.0 - peclet_y),
            jnp.where(column == 0, 0.0, rate * (1.0 + peclet_x)),
            jnp.where(column == cols - 1, 0.0, rate * (1.0 - peclet_x)),
            step_scale * source * share,
        ],
        0,
    )


def sweep(fields, halo, count, spread, with_source):
    n, rows, cols = fields.shape
    kernel = functools.partial(_sweep_kernel, count, with_source, COEFF_HALO - halo)
    return pl.pallas_call(
        kernel,
        out_shape=jax.ShapeDtypeStruct((n, rows - 2 * count, cols), jnp.float32),
        in_specs=[pl.BlockSpec(memory_space=pltpu.VMEM)] * 2,
        out_specs=pl.BlockSpec(memory_space=pltpu.VMEM),
        scratch_shapes=[pltpu.VMEM((2, rows + 2 * PAD, cols), jnp.float32)],
        cost_estimate=pl.CostEstimate(
            flops=12 * n * rows * cols * count, transcendentals=0, bytes_accessed=4 * (n + 6) * rows * cols
        ),
    )(fields, spread)


def _level_kernel(halo, first, defect_ref, b_ref, prev_ref, mine_ref, buf, outgoing, send_sems, recv_sems):
    rows, cols = defect_ref.shape
    span = rows + 2 * halo
    me_t, me_s = lax.axis_index("tm"), lax.axis_index("space")
    tms, sps = lax.axis_size("tm"), lax.axis_size("space")

    def inside(t, s):
        return (t >= 0) & (t < tms) & (s >= 0) & (s < sps)

    buf[:, 0:PAD, :] = jnp.zeros((2, PAD, cols), jnp.float32)
    buf[:, PAD + span : 2 * PAD + span, :] = jnp.zeros((2, PAD, cols), jnp.float32)
    routes = (
        ((halo, halo + rows), (0, rows), (1, 0)),
        ((0, halo), (rows - halo, rows), (1, 1)),
        ((halo + rows, span), (0, halo), (1, -1)),
    )
    for (a, b), _, (dt, ds) in routes:
        @pl.when(jnp.logical_not(inside(me_t - dt, me_s - ds)))
        def _():
            buf[0, PAD + a : PAD + b, :] = jnp.zeros((b - a, cols), jnp.float32)

    partners = [(dt, ds) for _, _, (dt, ds) in routes] + [(-dt, -ds) for _, _, (dt, ds) in routes]
    barrier = pltpu.get_barrier_semaphore()
    peers = 0
    for dt, ds in partners:
        @pl.when(inside(me_t + dt, me_s + ds))
        def _():
            pl.semaphore_signal(
                barrier, 1, device_id=(me_t + dt, me_s + ds), device_id_type=MESH
            )
        peers = peers + _present(me_t, dt, tms) * _present(me_s, ds, sps)
    pl.semaphore_wait(barrier, peers)

    copies = []
    for slot, ((a, b), (c, d), (dt, ds)) in enumerate(routes):
        incoming = pltpu.make_async_remote_copy(
            src_ref=outgoing.at[pl.ds(c, d - c)],
            dst_ref=buf.at[0, pl.ds(PAD + a, b - a)],
            send_sem=send_sems.at[slot],
            recv_sem=recv_sems.at[slot],
            device_id=(me_t - dt, me_s - ds),
            device_id_type=MESH,
        )

        @pl.when(inside(me_t - dt, me_s - ds))
        def _():
            incoming.wait_recv()

        copies.append(
            pltpu.make_async_remote_copy(
                src_ref=outgoing.at[pl.ds(c, d - c)],
                dst_ref=buf.at[0, pl.ds(PAD + a, b - a)],
                send_sem=send_sems.at[slot],
                recv_sem=recv_sems.at[slot],
                device_id=(me_t + dt, me_s + ds),
                device_id_type=MESH,
            )
        )

    prev_ref[...] = buf[0, PAD : PAD + span, :]
    for step in range(SUBSTEPS // 2):
        _stencil(buf, b_ref, first, span, cols, 0, 1, False)
        _stencil(buf, b_ref, first, span, cols, 1, 0, False)
    mine = buf[0, PAD + halo : PAD + halo + rows, :] + defect_ref[...]
    mine_ref[...] = mine
    outgoing[...] = mine
    for copy, (_, _, (dt, ds)) in zip(copies, routes):
        @pl.when(inside(me_t + dt, me_s + ds))
        def _():
            copy.start()
    for copy, (_, _, (dt, ds)) in zip(copies, routes):
        @pl.when(inside(me_t + dt, me_s + ds))
        def _():
            copy.wait_send()


def level_chain(defect, spread, halo, cid):
    rows, cols = defect.shape
    span = rows + 2 * halo
    kernel = functools.partial(_level_kernel, halo, COEFF_HALO - halo)
    return pl.pallas_call(
        kernel,
        out_shape=[
            jax.ShapeDtypeStruct((span, cols), jnp.float32),
            jax.ShapeDtypeStruct((rows, cols), jnp.float32),
        ],
        in_specs=[pl.BlockSpec(memory_space=pltpu.VMEM)] * 2,
        out_specs=[pl.BlockSpec(memory_space=pltpu.VMEM)] * 2,
        scratch_shapes=[
            pltpu.VMEM((2, span + 2 * PAD, cols), jnp.float32),
            pltpu.VMEM((rows, cols), jnp.float32),
            pltpu.SemaphoreType.DMA((3,)),
            pltpu.SemaphoreType.DMA((3,)),
        ],
        compiler_params=pltpu.CompilerParams(collective_id=cid, has_side_effects=True),
    )(defect, spread)


def moved(x, dt, ds):
    tms, sps = lax.axis_size("tm"), lax.axis_size("space")
    pairs = [
        (t * sps + s, (t + dt) * sps + (s + ds))
        for t in range(tms)
        for s in range(sps)
        if 0 <= t + dt < tms and 0 <= s + ds < sps
    ]
    return lax.ppermute(x, ("tm", "space"), pairs)


def with_halo(block, width, dt=0):
    rows = block.shape[-2]
    low = moved(block[..., rows - width :, :], dt, 1)
    high = moved(block[..., :width, :], dt, -1)
    middle = block if dt == 0 else moved(block, dt, 0)
    return jnp.concatenate([low, middle, high], axis=-2)


def trim(x, halo, keep):
    return x[..., halo - keep : x.shape[-2] - halo + keep, :]


def substep(extended, window, step_scale, with_source):
    middle = extended[..., 1:-1, :]
    north_row = extended[..., :-2, :]
    south_row = extended[..., 2:, :]
    widths = [(0, 0)] * (middle.ndim - 1) + [(1, 1)]
    padded = jnp.pad(middle, widths)
    west_col = padded[..., :-2]
    east_col = padded[..., 2:]
    rate_field = window[0]
    inflow = rate_field * (
        north_row
        + south_row
        + west_col
        + east_col
        + window[1] * (west_col - east_col)
        + window[2] * (north_row - south_row)
    )
    if with_source:
        inflow = inflow + window[3]
    return (middle + step_scale * inflow) / (1.0 + 4.0 * step_scale * rate_field)


def advance(fields, halo, count, coeffs, step_scale, with_source):
    inner = coeffs.shape[-2] - 2 * COEFF_HALO
    for position in range(count):
        out_halo = halo - position - 1
        first = COEFF_HALO - out_halo
        window = coeffs[:, first : first + inner + 2 * out_halo, :]
        fields = substep(fields, window, step_scale, with_source)
    return fields


def on_device(start_field, guessed, diffusion, peclet_x, peclet_y, source):
    rows, cols = start_field.shape
    R, H, L, h = rows, COEFF_HALO, LEVEL_HALO, SWEEP
    F = fixed_rows
    stacked = jnp.stack([diffusion, peclet_x, peclet_y, source], 0)
    first_points = [
        (0, (slice(0, 3), slice(0, R)), 0, F((slice(1, 4), slice(h, h + R))), None, False),
        (0, (slice(0, 3), slice(R - h, R)), 0, F((slice(1, 4), slice(0, h))), (0, 1), False),
        (0, (slice(0, 3), slice(0, h)), 0, F((slice(1, 4), slice(h + R, 2 * h + R))), (0, -1), False),
        (0, (3, slice(0, R)), 0, F((0, slice(h, h + R))), (1, 0), False),
        (0, (3, slice(R - h, R)), 0, F((0, slice(0, h))), (1, 1), False),
        (0, (3, slice(0, h)), 0, F((0, slice(h + R, 2 * h + R))), (1, -1), False),
        (1, (slice(0, R),), 1, F((slice(H, H + R),)), None, False),
        (1, (slice(R - H, R),), 1, F((slice(0, H),)), (0, 1), False),
        (1, (slice(0, H),), 1, F((slice(H + R, 2 * H + R),)), (0, -1), False),
        (2, (slice(0, 4), slice(0, R)), 2, F((slice(0, 4), slice(H, H + R))), None, False),
        (2, (slice(0, 4), slice(R - H, R)), 2, F((slice(0, 4), slice(0, H))), (0, 1), False),
        (2, (slice(0, 4), slice(0, H)), 2, F((slice(0, 4), slice(H + R, 2 * H + R))), (0, -1), False),
    ]
    ext1, start_ext, coeffs = exchange(
        [guessed, start_field, stacked],
        [(4, 2 * h + R, cols), (2 * H + R, cols), (4, 2 * H + R, cols)],
        first_points,
        1,
    )
    my_index = lax.axis_index("tm")
    first_slab = my_index == 0
    level_scale = float(COARSEN_ONE)
    top_scale = float(COARSEN_ONE * COARSEN_TWO)

    opening = jnp.where(first_slab, trim(start_ext, H, h), ext1[0])
    before1 = jnp.concatenate([opening[None], ext1[1:]], 0)
    fine = weights(coeffs, 1.0)
    settled = sweep(before1, h, SWEEP, fine, True)

    second_points = [
        (0, (slice(0, 4), slice(0, R)), 0, F((slice(1, 5), slice(H, H + R))), None, False),
        (0, (slice(0, 4), slice(R - H, R)), 0, F((slice(1, 5), slice(0, H))), (0, 1), False),
        (0, (slice(0, 4), slice(0, H)), 0, F((slice(1, 5), slice(H + R, 2 * H + R))), (0, -1), False),
        (0, (3, slice(0, R)), 0, F((0, slice(H, H + R))), (1, 0), False),
        (0, (3, slice(R - H, R)), 0, F((0, slice(0, H))), (1, 1), False),
        (0, (3, slice(0, H)), 0, F((0, slice(H + R, 2 * H + R))), (1, -1), False),
    ]
    (ext2,) = exchange([settled], [(5, 2 * H + R, cols)], second_points, 2)
    opening = jnp.where(first_slab, start_ext, ext2[0])
    before2 = jnp.concatenate([opening[None], ext2[1:4]], 0)
    swept = sweep(before2, H, SWEEP, fine, True)
    residual = swept - trim(ext2[1:5], H, H - SWEEP)
    stored = H - SWEEP

    def coarse(x, halo):
        return advance(x, halo, SUBSTEPS, coeffs, level_scale, False)

    def r_at(position, keep):
        return trim(residual[position], stored, keep)

    running = r_at(0, RES_HALO)
    halo = RES_HALO
    for position in range(1, COARSEN_TWO):
        running = coarse(running, halo) + r_at(position, halo - SUBSTEPS)
        halo -= SUBSTEPS
    c_value = running

    e = 4 * SUBSTEPS
    shift_points = [
        (0, (slice(0, R),), 0, F((slice(e, e + R),)), (1, 0), False),
        (0, (slice(R - e, R),), 0, F((slice(0, e),)), (1, 1), False),
        (0, (slice(0, e),), 0, F((slice(e + R, 2 * e + R),)), (1, -1), False),
    ]
    (entering,) = exchange([c_value], [(2 * e + R, cols)], shift_points, 3)
    running = entering
    halo = e
    for position in range(COARSEN_TWO - 1):
        running = coarse(running, halo) + r_at(position, halo - SUBSTEPS)
        halo -= SUBSTEPS
    defect = (r_at(COARSEN_TWO - 1, 0) + coarse(running, halo)) - c_value

    level_halo = 16
    prev_level, mine = level_chain(defect, weights(coeffs, top_scale), level_halo, 4)
    level_before = trim(prev_level, level_halo, RES_HALO)

    c_fixed = c_value + mine
    running = jnp.where(first_slab, 0.0, trim(entering, e, RES_HALO) + level_before)
    halo = RES_HALO
    pieces = []
    for position in range(COARSEN_TWO - 1):
        running = coarse(running, halo) + r_at(position, halo - SUBSTEPS)
        halo -= SUBSTEPS
        pieces.append(trim(running, halo, 0))
    pieces.append(c_fixed)
    return settled + jnp.stack(pieces, 0)


def solution(mesh):
    in_specs = (
        P("space", None),
        P("tm", "space", None),
        P("space", None),
        P("space", None),
        P("space", None),
        P("space", None),
    )
    out_specs = P("tm", "space", None)
    return jax.shard_map(
        on_device, mesh=mesh, in_specs=in_specs, out_specs=out_specs, check_vma=False
    )
```

```python
import functools

import jax
import jax.numpy as jnp
import numpy as np
from jax import lax
from jax.experimental import pallas as pl
from jax.experimental.pallas import tpu as pltpu
from jax.sharding import PartitionSpec as P

MESH = pl.DeviceIdType.MESH

SUBSTEPS = 4
COARSEN_ONE = 8
COARSEN_TWO = 4
SWEEP = SUBSTEPS * COARSEN_ONE
COEFF_HALO = 48
RES_HALO = 3 * SUBSTEPS
LEVEL_HALO = 40


def _shape_of(shape, index):
    return np.broadcast_to(np.float32(0), shape)[index].shape


def _present(index, offset, size):
    if offset >= 0:
        return 1 - (index + offset) // size
    return (index + offset + size) // size


def _exchange_kernel(n_in, n_out, entries, partners, fill_outs, zero_shape, *refs):
    ins = refs[:n_in]
    outs = refs[n_in : n_in + n_out]
    zeros, send_sems, recv_sems, local_sems, fill_sems, back_sems = refs[n_in + n_out :]
    me_t, me_s = lax.axis_index("tm"), lax.axis_index("space")
    tms, sps = lax.axis_size("tm"), lax.axis_size("space")

    def inside(t, s):
        return (t >= 0) & (t < tms) & (s >= 0) & (s < sps)

    def zero_view(shape):
        lead = (0,) * (3 - len(shape))
        return zeros.at[lead + tuple(slice(0, n) for n in shape)]

    zeros[...] = jnp.zeros_like(zeros)
    barrier = pltpu.get_barrier_semaphore()
    for dt, ds in partners:
        @pl.when(inside(me_t + dt, me_s + ds))
        def _():
            pl.semaphore_signal(
                barrier, 1, device_id=(me_t + dt, me_s + ds), device_id_type=MESH
            )
    peers = 0
    for dt, ds in partners:
        peers = peers + _present(me_t, dt, tms) * _present(me_s, ds, sps)
    pl.semaphore_wait(barrier, peers)

    remote = [e for e in entries if e[4] is not None]
    sends = []
    for slot, (src, src_index, dst, dst_index, offset, dynamic) in enumerate(remote):
        dt, ds = offset
        copy = pltpu.make_async_remote_copy(
            src_ref=ins[src].at[src_index],
            dst_ref=outs[dst].at[dst_index(me_t)],
            send_sem=send_sems.at[slot],
            recv_sem=recv_sems.at[slot],
            device_id=(me_t + dt, me_s + ds),
            device_id_type=MESH,
        )
        target = inside(me_t + dt, me_s + ds)

        @pl.when(target)
        def _():
            copy.start()

        sends.append((copy, target))

    locals_ = []
    for src, src_index, dst, dst_index, offset, dynamic in entries:
        if offset is not None:
            continue
        copy = pltpu.make_async_copy(
            ins[src].at[src_index], outs[dst].at[dst_index(me_t)], local_sems.at[len(locals_)]
        )
        copy.start()
        locals_.append(copy)

    fills = []
    for dst in fill_outs:
        for k in range(outs[dst].shape[0]):
            fill = pltpu.make_async_copy(
                zero_view(outs[dst].shape[1:]), outs[dst].at[k], fill_sems.at[len(fills)]
            )

            @pl.when(k > me_t)
            def _():
                fill.start()

            fills.append((k, fill))

    for slot, (src, src_index, dst, dst_index, offset, dynamic) in enumerate(remote):
        dt, ds = offset
        sender_t, sender_s = me_t - dt, me_s - ds
        has_sender = inside(sender_t, sender_s)
        incoming = pltpu.make_async_remote_copy(
            src_ref=ins[src].at[src_index],
            dst_ref=outs[dst].at[dst_index(sender_t)],
            send_sem=send_sems.at[slot],
            recv_sem=recv_sems.at[slot],
            device_id=(sender_t, sender_s),
            device_id_type=MESH,
        )

        @pl.when(has_sender)
        def _():
            incoming.wait_recv()

        missing = jnp.logical_not(has_sender)
        if dynamic:
            missing = missing & (sender_t >= 0) & (sender_t < tms)
        fallback = pltpu.make_async_copy(
            zero_view(_shape_of(ins[src].shape, src_index)),
            outs[dst].at[dst_index(sender_t)],
            back_sems.at[slot],
        )

        @pl.when(missing)
        def _():
            fallback.start()
            fallback.wait()

    for copy in locals_:
        copy.wait()
    for k, fill in fills:
        @pl.when(k > me_t)
        def _():
            fill.wait()
    for copy, target in sends:
        @pl.when(target)
        def _():
            copy.wait_send()


def exchange(inputs, out_shapes, entries, cid, fill_outs=()):
    partners = []
    for entry in entries:
        if entry[4] is None:
            continue
        dt, ds = entry[4]
        for o in ((dt, ds), (-dt, -ds)):
            if o not in partners:
                partners.append(o)
    shapes = [_shape_of(inputs[e[0]].shape, e[1]) for e in entries]
    shapes += [tuple(out_shapes[dst][1:]) for dst in fill_outs]
    padded = [(1,) * (3 - len(s)) + tuple(s) for s in shapes]
    zero_shape = tuple(max(s[i] for s in padded) for i in range(3))
    n_remote = sum(e[4] is not None for e in entries)
    n_local = sum(e[4] is None for e in entries)
    n_fill = sum(out_shapes[dst][0] for dst in fill_outs)
    kernel = functools.partial(
        _exchange_kernel,
        len(inputs),
        len(out_shapes),
        tuple(entries),
        tuple(partners),
        tuple(fill_outs),
        zero_shape,
    )
    return pl.pallas_call(
        kernel,
        out_shape=[jax.ShapeDtypeStruct(s, jnp.float32) for s in out_shapes],
        in_specs=[pl.BlockSpec(memory_space=pltpu.VMEM)] * len(inputs),
        out_specs=[pl.BlockSpec(memory_space=pl.ANY)] * len(out_shapes),
        scratch_shapes=[
            pltpu.VMEM(zero_shape, jnp.float32),
            pltpu.SemaphoreType.DMA((max(n_remote, 1),)),
            pltpu.SemaphoreType.DMA((max(n_remote, 1),)),
            pltpu.SemaphoreType.DMA((max(n_local, 1),)),
            pltpu.SemaphoreType.DMA((max(n_fill, 1),)),
            pltpu.SemaphoreType.DMA((max(n_remote, 1),)),
        ],
        compiler_params=pltpu.CompilerParams(collective_id=cid, has_side_effects=True),
    )(*inputs)


def fixed_rows(index):
    return lambda sender: index


CHUNK = 16
PAD = 8


def _stencil(buf, b_ref, first, rows, cols, src, dst, with_source):
    for c0 in range(0, rows, CHUNK):
        def weight(k):
            return b_ref[k, pl.ds(first + c0, CHUNK), :]

        centre = buf[src, pl.ds(PAD + c0, CHUNK), :]
        north_row = buf[src, pl.ds(PAD + c0 - 1, CHUNK), :]
        south_row = buf[src, pl.ds(PAD + c0 + 1, CHUNK), :]
        west_col = pltpu.roll(centre, 1, 1)
        east_col = pltpu.roll(centre, cols - 1, 1)
        new = (
            weight(0) * centre
            + weight(1) * north_row
            + weight(2) * south_row
            + weight(3) * west_col
            + weight(4) * east_col
        )
        if with_source:
            new = new + weight(5)
        buf[dst, pl.ds(PAD + c0, CHUNK), :] = new


def _sweep_kernel(count, with_source, first, x_ref, b_ref, o_ref, buf):
    fields, rows, cols = x_ref.shape
    buf[:, 0:PAD, :] = jnp.zeros((2, PAD, cols), jnp.float32)
    buf[:, PAD + rows : 2 * PAD + rows, :] = jnp.zeros((2, PAD, cols), jnp.float32)

    def two(step, carry):
        _stencil(buf, b_ref, first, rows, cols, 0, 1, with_source)
        _stencil(buf, b_ref, first, rows, cols, 1, 0, with_source)
        return carry

    for f in range(fields):
        buf[0, PAD : PAD + rows, :] = x_ref[f]
        lax.fori_loop(0, count // 2, two, 0, unroll=4)
        o_ref[f] = buf[0, pl.ds(PAD + count, rows - 2 * count), :]


def weights(coeffs, step_scale):
    diffusion, peclet_x, peclet_y, source = coeffs
    share = 1.0 / (1.0 + 4.0 * step_scale * diffusion)
    rate = step_scale * diffusion * share
    column = lax.broadcasted_iota(jnp.int32, diffusion.shape, diffusion.ndim - 1)
    cols = diffusion.shape[-1]
    return jnp.stack(
        [
            share,
            rate * (1.0 + peclet_y),
            rate * (1.0 - peclet_y),
            jnp.where(column == 0, 0.0, rate * (1.0 + peclet_x)),
            jnp.where(column == cols - 1, 0.0, rate * (1.0 - peclet_x)),
            step_scale * source * share,
        ],
        0,
    )


def sweep(fields, halo, count, spread, with_source):
    n, rows, cols = fields.shape
    kernel = functools.partial(_sweep_kernel, count, with_source, COEFF_HALO - halo)
    return pl.pallas_call(
        kernel,
        out_shape=jax.ShapeDtypeStruct((n, rows - 2 * count, cols), jnp.float32),
        in_specs=[pl.BlockSpec(memory_space=pltpu.VMEM)] * 2,
        out_specs=pl.BlockSpec(memory_space=pltpu.VMEM),
        scratch_shapes=[pltpu.VMEM((2, rows + 2 * PAD, cols), jnp.float32)],
        cost_estimate=pl.CostEstimate(
            flops=12 * n * rows * cols * count, transcendentals=0, bytes_accessed=4 * (n + 6) * rows * cols
        ),
    )(fields, spread)


def _level_kernel(halo, first, defect_ref, b_ref, prev_ref, mine_ref, buf, outgoing, send_sems, recv_sems):
    rows, cols = defect_ref.shape
    span = rows + 2 * halo
    me_t, me_s = lax.axis_index("tm"), lax.axis_index("space")
    tms, sps = lax.axis_size("tm"), lax.axis_size("space")

    def inside(t, s):
        return (t >= 0) & (t < tms) & (s >= 0) & (s < sps)

    buf[:, 0:PAD, :] = jnp.zeros((2, PAD, cols), jnp.float32)
    buf[:, PAD + span : 2 * PAD + span, :] = jnp.zeros((2, PAD, cols), jnp.float32)
    routes = (
        ((halo, halo + rows), (0, rows), (1, 0)),
        ((0, halo), (rows - halo, rows), (1, 1)),
        ((halo + rows, span), (0, halo), (1, -1)),
    )
    for (a, b), _, (dt, ds) in routes:
        @pl.when(jnp.logical_not(inside(me_t - dt, me_s - ds)))
        def _():
            buf[0, PAD + a : PAD + b, :] = jnp.zeros((b - a, cols), jnp.float32)

    partners = [(dt, ds) for _, _, (dt, ds) in routes] + [(-dt, -ds) for _, _, (dt, ds) in routes]
    barrier = pltpu.get_barrier_semaphore()
    peers = 0
    for dt, ds in partners:
        @pl.when(inside(me_t + dt, me_s + ds))
        def _():
            pl.semaphore_signal(
                barrier, 1, device_id=(me_t + dt, me_s + ds), device_id_type=MESH
            )
        peers = peers + _present(me_t, dt, tms) * _present(me_s, ds, sps)
    pl.semaphore_wait(barrier, peers)

    copies = []
    for slot, ((a, b), (c, d), (dt, ds)) in enumerate(routes):
        incoming = pltpu.make_async_remote_copy(
            src_ref=outgoing.at[pl.ds(c, d - c)],
            dst_ref=buf.at[0, pl.ds(PAD + a, b - a)],
            send_sem=send_sems.at[slot],
            recv_sem=recv_sems.at[slot],
            device_id=(me_t - dt, me_s - ds),
            device_id_type=MESH,
        )

        @pl.when(inside(me_t - dt, me_s - ds))
        def _():
            incoming.wait_recv()

        copies.append(
            pltpu.make_async_remote_copy(
                src_ref=outgoing.at[pl.ds(c, d - c)],
                dst_ref=buf.at[0, pl.ds(PAD + a, b - a)],
                send_sem=send_sems.at[slot],
                recv_sem=recv_sems.at[slot],
                device_id=(me_t + dt, me_s + ds),
                device_id_type=MESH,
            )
        )

    prev_ref[...] = buf[0, PAD : PAD + span, :]
    for step in range(SUBSTEPS // 2):
        _stencil(buf, b_ref, first, span, cols, 0, 1, False)
        _stencil(buf, b_ref, first, span, cols, 1, 0, False)
    mine = buf[0, PAD + halo : PAD + halo + rows, :] + defect_ref[...]
    mine_ref[...] = mine
    outgoing[...] = mine
    for copy, (_, _, (dt, ds)) in zip(copies, routes):
        @pl.when(inside(me_t + dt, me_s + ds))
        def _():
            copy.start()
    for copy, (_, _, (dt, ds)) in zip(copies, routes):
        @pl.when(inside(me_t + dt, me_s + ds))
        def _():
            copy.wait_send()


def level_chain(defect, spread, halo, cid):
    rows, cols = defect.shape
    span = rows + 2 * halo
    kernel = functools.partial(_level_kernel, halo, COEFF_HALO - halo)
    return pl.pallas_call(
        kernel,
        out_shape=[
            jax.ShapeDtypeStruct((span, cols), jnp.float32),
            jax.ShapeDtypeStruct((rows, cols), jnp.float32),
        ],
        in_specs=[pl.BlockSpec(memory_space=pltpu.VMEM)] * 2,
        out_specs=[pl.BlockSpec(memory_space=pltpu.VMEM)] * 2,
        scratch_shapes=[
            pltpu.VMEM((2, span + 2 * PAD, cols), jnp.float32),
            pltpu.VMEM((rows, cols), jnp.float32),
            pltpu.SemaphoreType.DMA((3,)),
            pltpu.SemaphoreType.DMA((3,)),
        ],
        compiler_params=pltpu.CompilerParams(collective_id=cid, has_side_effects=True),
    )(defect, spread)


def moved(x, dt, ds):
    tms, sps = lax.axis_size("tm"), lax.axis_size("space")
    pairs = [
        (t * sps + s, (t + dt) * sps + (s + ds))
        for t in range(tms)
        for s in range(sps)
        if 0 <= t + dt < tms and 0 <= s + ds < sps
    ]
    return lax.ppermute(x, ("tm", "space"), pairs)


def with_halo(block, width, dt=0):
    rows = block.shape[-2]
    low = moved(block[..., rows - width :, :], dt, 1)
    high = moved(block[..., :width, :], dt, -1)
    middle = block if dt == 0 else moved(block, dt, 0)
    return jnp.concatenate([low, middle, high], axis=-2)


def trim(x, halo, keep):
    return x[..., halo - keep : x.shape[-2] - halo + keep, :]


def substep(extended, window, step_scale, with_source):
    middle = extended[..., 1:-1, :]
    north_row = extended[..., :-2, :]
    south_row = extended[..., 2:, :]
    widths = [(0, 0)] * (middle.ndim - 1) + [(1, 1)]
    padded = jnp.pad(middle, widths)
    west_col = padded[..., :-2]
    east_col = padded[..., 2:]
    rate_field = window[0]
    inflow = rate_field * (
        north_row
        + south_row
        + west_col
        + east_col
        + window[1] * (west_col - east_col)
        + window[2] * (north_row - south_row)
    )
    if with_source:
        inflow = inflow + window[3]
    return (middle + step_scale * inflow) / (1.0 + 4.0 * step_scale * rate_field)


def advance(fields, halo, count, coeffs, step_scale, with_source):
    inner = coeffs.shape[-2] - 2 * COEFF_HALO
    for position in range(count):
        out_halo = halo - position - 1
        first = COEFF_HALO - out_halo
        window = coeffs[:, first : first + inner + 2 * out_halo, :]
        fields = substep(fields, window, step_scale, with_source)
    return fields


def on_device(start_field, guessed, diffusion, peclet_x, peclet_y, source):
    rows, cols = start_field.shape
    R, H, L, h = rows, COEFF_HALO, LEVEL_HALO, SWEEP
    F = fixed_rows
    stacked = jnp.stack([diffusion, peclet_x, peclet_y, source], 0)
    first_points = [
        (0, (slice(0, 3), slice(0, R)), 0, F((slice(1, 4), slice(h, h + R))), None, False),
        (0, (slice(0, 3), slice(R - h, R)), 0, F((slice(1, 4), slice(0, h))), (0, 1), False),
        (0, (slice(0, 3), slice(0, h)), 0, F((slice(1, 4), slice(h + R, 2 * h + R))), (0, -1), False),
        (0, (3, slice(0, R)), 0, F((0, slice(h, h + R))), (1, 0), False),
        (0, (3, slice(R - h, R)), 0, F((0, slice(0, h))), (1, 1), False),
        (0, (3, slice(0, h)), 0, F((0, slice(h + R, 2 * h + R))), (1, -1), False),
        (1, (slice(0, R),), 1, F((slice(H, H + R),)), None, False),
        (1, (slice(R - H, R),), 1, F((slice(0, H),)), (0, 1), False),
        (1, (slice(0, H),), 1, F((slice(H + R, 2 * H + R),)), (0, -1), False),
        (2, (slice(0, 4), slice(0, R)), 2, F((slice(0, 4), slice(H, H + R))), None, False),
        (2, (slice(0, 4), slice(R - H, R)), 2, F((slice(0, 4), slice(0, H))), (0, 1), False),
        (2, (slice(0, 4), slice(0, H)), 2, F((slice(0, 4), slice(H + R, 2 * H + R))), (0, -1), False),
    ]
    ext1, start_ext, coeffs = exchange(
        [guessed, start_field, stacked],
        [(4, 2 * h + R, cols), (2 * H + R, cols), (4, 2 * H + R, cols)],
        first_points,
        1,
    )
    my_index = lax.axis_index("tm")
    first_slab = my_index == 0
    level_scale = float(COARSEN_ONE)
    top_scale = float(COARSEN_ONE * COARSEN_TWO)

    opening = jnp.where(first_slab, trim(start_ext, H, h), ext1[0])
    before1 = jnp.concatenate([opening[None], ext1[1:]], 0)
    fine = weights(coeffs, 1.0)
    settled = sweep(before1, h, SWEEP, fine, True)

    second_points = [
        (0, (slice(0, 4), slice(0, R)), 0, F((slice(1, 5), slice(H, H + R))), None, False),
        (0, (slice(0, 4), slice(R - H, R)), 0, F((slice(1, 5), slice(0, H))), (0, 1), False),
        (0, (slice(0, 4), slice(0, H)), 0, F((slice(1, 5), slice(H + R, 2 * H + R))), (0, -1), False),
        (0, (3, slice(0, R)), 0, F((0, slice(H, H + R))), (1, 0), False),
        (0, (3, slice(R - H, R)), 0, F((0, slice(0, H))), (1, 1), False),
        (0, (3, slice(0, H)), 0, F((0, slice(H + R, 2 * H + R))), (1, -1), False),
    ]
    (ext2,) = exchange([settled], [(5, 2 * H + R, cols)], second_points, 2)
    opening = jnp.where(first_slab, start_ext, ext2[0])
    before2 = jnp.concatenate([opening[None], ext2[1:4]], 0)
    swept = sweep(before2, H, SWEEP, fine, True)
    residual = swept - trim(ext2[1:5], H, H - SWEEP)
    stored = H - SWEEP

    def coarse(x, halo):
        return advance(x, halo, SUBSTEPS, coeffs, level_scale, False)

    def r_at(position, keep):
        return trim(residual[position], stored, keep)

    running = r_at(0, RES_HALO)
    halo = RES_HALO
    for position in range(1, COARSEN_TWO):
        running = coarse(running, halo) + r_at(position, halo - SUBSTEPS)
        halo -= SUBSTEPS
    c_value = running

    e = 4 * SUBSTEPS
    shift_points = [
        (0, (slice(0, R),), 0, F((slice(e, e + R),)), (1, 0), False),
        (0, (slice(R - e, R),), 0, F((slice(0, e),)), (1, 1), False),
        (0, (slice(0, e),), 0, F((slice(e + R, 2 * e + R),)), (1, -1), False),
    ]
    (entering,) = exchange([c_value], [(2 * e + R, cols)], shift_points, 3)
    running = entering
    halo = e
    for position in range(COARSEN_TWO - 1):
        running = coarse(running, halo) + r_at(position, halo - SUBSTEPS)
        halo -= SUBSTEPS
    defect = (r_at(COARSEN_TWO - 1, 0) + coarse(running, halo)) - c_value

    level_halo = 16
    prev_level, mine = level_chain(defect, weights(coeffs, top_scale), level_halo, 4)
    level_before = trim(prev_level, level_halo, RES_HALO)

    c_fixed = c_value + mine
    running = jnp.where(first_slab, 0.0, trim(entering, e, RES_HALO) + level_before)
    halo = RES_HALO
    pieces = []
    for position in range(COARSEN_TWO - 1):
        running = coarse(running, halo) + r_at(position, halo - SUBSTEPS)
        halo -= SUBSTEPS
        pieces.append(trim(running, halo, 0))
    pieces.append(c_fixed)
    return settled + jnp.stack(pieces, 0)


def solution(mesh):
    in_specs = (
        P("space", None),
        P("tm", "space", None),
        P("space", None),
        P("space", None),
        P("space", None),
        P("space", None),
    )
    out_specs = P("tm", "space", None)
    return jax.shard_map(
        on_device, mesh=mesh, in_specs=in_specs, out_specs=out_specs, check_vma=False
    )
```

```python
import functools

import jax
import jax.numpy as jnp
import numpy as np
from jax import lax
from jax.experimental import pallas as pl
from jax.experimental.pallas import tpu as pltpu
from jax.sharding import PartitionSpec as P

MESH = pl.DeviceIdType.MESH

SUBSTEPS = 4
COARSEN_ONE = 8
COARSEN_TWO = 4
SWEEP = SUBSTEPS * COARSEN_ONE
COEFF_HALO = 48
RES_HALO = 3 * SUBSTEPS
LEVEL_HALO = 40


def _shape_of(shape, index):
    return np.broadcast_to(np.float32(0), shape)[index].shape


def _present(index, offset, size):
    if offset >= 0:
        return 1 - (index + offset) // size
    return (index + offset + size) // size


def _exchange_kernel(n_in, n_out, entries, partners, fill_outs, zero_shape, *refs):
    ins = refs[:n_in]
    outs = refs[n_in : n_in + n_out]
    zeros, send_sems, recv_sems, local_sems, fill_sems, back_sems = refs[n_in + n_out :]
    me_t, me_s = lax.axis_index("tm"), lax.axis_index("space")
    tms, sps = lax.axis_size("tm"), lax.axis_size("space")

    def inside(t, s):
        return (t >= 0) & (t < tms) & (s >= 0) & (s < sps)

    def zero_view(shape):
        lead = (0,) * (3 - len(shape))
        return zeros.at[lead + tuple(slice(0, n) for n in shape)]

    zeros[...] = jnp.zeros_like(zeros)
    barrier = pltpu.get_barrier_semaphore()
    for dt, ds in partners:
        @pl.when(inside(me_t + dt, me_s + ds))
        def _():
            pl.semaphore_signal(
                barrier, 1, device_id=(me_t + dt, me_s + ds), device_id_type=MESH
            )
    peers = 0
    for dt, ds in partners:
        peers = peers + _present(me_t, dt, tms) * _present(me_s, ds, sps)
    pl.semaphore_wait(barrier, peers)

    remote = [e for e in entries if e[4] is not None]
    sends = []
    for slot, (src, src_index, dst, dst_index, offset, dynamic) in enumerate(remote):
        dt, ds = offset
        copy = pltpu.make_async_remote_copy(
            src_ref=ins[src].at[src_index],
            dst_ref=outs[dst].at[dst_index(me_t)],
            send_sem=send_sems.at[slot],
            recv_sem=recv_sems.at[slot],
            device_id=(me_t + dt, me_s + ds),
            device_id_type=MESH,
        )
        target = inside(me_t + dt, me_s + ds)

        @pl.when(target)
        def _():
            copy.start()

        sends.append((copy, target))

    locals_ = []
    for src, src_index, dst, dst_index, offset, dynamic in entries:
        if offset is not None:
            continue
        copy = pltpu.make_async_copy(
            ins[src].at[src_index], outs[dst].at[dst_index(me_t)], local_sems.at[len(locals_)]
        )
        copy.start()
        locals_.append(copy)

    fills = []
    for dst in fill_outs:
        for k in range(outs[dst].shape[0]):
            fill = pltpu.make_async_copy(
                zero_view(outs[dst].shape[1:]), outs[dst].at[k], fill_sems.at[len(fills)]
            )

            @pl.when(k > me_t)
            def _():
                fill.start()

            fills.append((k, fill))

    for slot, (src, src_index, dst, dst_index, offset, dynamic) in enumerate(remote):
        dt, ds = offset
        sender_t, sender_s = me_t - dt, me_s - ds
        has_sender = inside(sender_t, sender_s)
        incoming = pltpu.make_async_remote_copy(
            src_ref=ins[src].at[src_index],
            dst_ref=outs[dst].at[dst_index(sender_t)],
            send_sem=send_sems.at[slot],
            recv_sem=recv_sems.at[slot],
            device_id=(sender_t, sender_s),
            device_id_type=MESH,
        )

        @pl.when(has_sender)
        def _():
            incoming.wait_recv()

        missing = jnp.logical_not(has_sender)
        if dynamic:
            missing = missing & (sender_t >= 0) & (sender_t < tms)
        fallback = pltpu.make_async_copy(
            zero_view(_shape_of(ins[src].shape, src_index)),
            outs[dst].at[dst_index(sender_t)],
            back_sems.at[slot],
        )

        @pl.when(missing)
        def _():
            fallback.start()
            fallback.wait()

    for copy in locals_:
        copy.wait()
    for k, fill in fills:
        @pl.when(k > me_t)
        def _():
            fill.wait()
    for copy, target in sends:
        @pl.when(target)
        def _():
            copy.wait_send()


def exchange(inputs, out_shapes, entries, cid, fill_outs=()):
    partners = []
    for entry in entries:
        if entry[4] is None:
            continue
        dt, ds = entry[4]
        for o in ((dt, ds), (-dt, -ds)):
            if o not in partners:
                partners.append(o)
    shapes = [_shape_of(inputs[e[0]].shape, e[1]) for e in entries]
    shapes += [tuple(out_shapes[dst][1:]) for dst in fill_outs]
    padded = [(1,) * (3 - len(s)) + tuple(s) for s in shapes]
    zero_shape = tuple(max(s[i] for s in padded) for i in range(3))
    n_remote = sum(e[4] is not None for e in entries)
    n_local = sum(e[4] is None for e in entries)
    n_fill = sum(out_shapes[dst][0] for dst in fill_outs)
    kernel = functools.partial(
        _exchange_kernel,
        len(inputs),
        len(out_shapes),
        tuple(entries),
        tuple(partners),
        tuple(fill_outs),
        zero_shape,
    )
    return pl.pallas_call(
        kernel,
        out_shape=[jax.ShapeDtypeStruct(s, jnp.float32) for s in out_shapes],
        in_specs=[pl.BlockSpec(memory_space=pltpu.VMEM)] * len(inputs),
        out_specs=[pl.BlockSpec(memory_space=pl.ANY)] * len(out_shapes),
        scratch_shapes=[
            pltpu.VMEM(zero_shape, jnp.float32),
            pltpu.SemaphoreType.DMA((max(n_remote, 1),)),
            pltpu.SemaphoreType.DMA((max(n_remote, 1),)),
            pltpu.SemaphoreType.DMA((max(n_local, 1),)),
            pltpu.SemaphoreType.DMA((max(n_fill, 1),)),
            pltpu.SemaphoreType.DMA((max(n_remote, 1),)),
        ],
        compiler_params=pltpu.CompilerParams(collective_id=cid, has_side_effects=True),
    )(*inputs)


def fixed_rows(index):
    return lambda sender: index


CHUNK = 8
PAD = 8


def _stencil(buf, b_ref, first, rows, cols, src, dst, with_source):
    for c0 in range(0, rows, CHUNK):
        def weight(k):
            return b_ref[k, pl.ds(first + c0, CHUNK), :]

        centre = buf[src, pl.ds(PAD + c0, CHUNK), :]
        north_row = buf[src, pl.ds(PAD + c0 - 1, CHUNK), :]
        south_row = buf[src, pl.ds(PAD + c0 + 1, CHUNK), :]
        west_col = pltpu.roll(centre, 1, 1)
        east_col = pltpu.roll(centre, cols - 1, 1)
        new = (
            weight(0) * centre
            + weight(1) * north_row
            + weight(2) * south_row
            + weight(3) * west_col
            + weight(4) * east_col
        )
        if with_source:
            new = new + weight(5)
        buf[dst, pl.ds(PAD + c0, CHUNK), :] = new


def _sweep_kernel(count, with_source, first, x_ref, b_ref, o_ref, buf):
    fields, rows, cols = x_ref.shape
    buf[:, 0:PAD, :] = jnp.zeros((2, PAD, cols), jnp.float32)
    buf[:, PAD + rows : 2 * PAD + rows, :] = jnp.zeros((2, PAD, cols), jnp.float32)

    def two(step, carry):
        _stencil(buf, b_ref, first, rows, cols, 0, 1, with_source)
        _stencil(buf, b_ref, first, rows, cols, 1, 0, with_source)
        return carry

    for f in range(fields):
        buf[0, PAD : PAD + rows, :] = x_ref[f]
        lax.fori_loop(0, count // 2, two, 0, unroll=2)
        o_ref[f] = buf[0, pl.ds(PAD + count, rows - 2 * count), :]


def weights(coeffs, step_scale):
    diffusion, peclet_x, peclet_y, source = coeffs
    share = 1.0 / (1.0 + 4.0 * step_scale * diffusion)
    rate = step_scale * diffusion * share
    column = lax.broadcasted_iota(jnp.int32, diffusion.shape, diffusion.ndim - 1)
    cols = diffusion.shape[-1]
    return jnp.stack(
        [
            share,
            rate * (1.0 + peclet_y),
            rate * (1.0 - peclet_y),
            jnp.where(column == 0, 0.0, rate * (1.0 + peclet_x)),
            jnp.where(column == cols - 1, 0.0, rate * (1.0 - peclet_x)),
            step_scale * source * share,
        ],
        0,
    )


def sweep(fields, halo, count, spread, with_source):
    n, rows, cols = fields.shape
    kernel = functools.partial(_sweep_kernel, count, with_source, COEFF_HALO - halo)
    return pl.pallas_call(
        kernel,
        out_shape=jax.ShapeDtypeStruct((n, rows - 2 * count, cols), jnp.float32),
        in_specs=[pl.BlockSpec(memory_space=pltpu.VMEM)] * 2,
        out_specs=pl.BlockSpec(memory_space=pltpu.VMEM),
        scratch_shapes=[pltpu.VMEM((2, rows + 2 * PAD, cols), jnp.float32)],
        cost_estimate=pl.CostEstimate(
            flops=12 * n * rows * cols * count, transcendentals=0, bytes_accessed=4 * (n + 6) * rows * cols
        ),
    )(fields, spread)


def _level_kernel(halo, first, defect_ref, b_ref, prev_ref, mine_ref, buf, outgoing, send_sems, recv_sems):
    rows, cols = defect_ref.shape
    span = rows + 2 * halo
    me_t, me_s = lax.axis_index("tm"), lax.axis_index("space")
    tms, sps = lax.axis_size("tm"), lax.axis_size("space")

    def inside(t, s):
        return (t >= 0) & (t < tms) & (s >= 0) & (s < sps)

    buf[:, 0:PAD, :] = jnp.zeros((2, PAD, cols), jnp.float32)
    buf[:, PAD + span : 2 * PAD + span, :] = jnp.zeros((2, PAD, cols), jnp.float32)
    routes = (
        ((halo, halo + rows), (0, rows), (1, 0)),
        ((0, halo), (rows - halo, rows), (1, 1)),
        ((halo + rows, span), (0, halo), (1, -1)),
    )
    for (a, b), _, (dt, ds) in routes:
        @pl.when(jnp.logical_not(inside(me_t - dt, me_s - ds)))
        def _():
            buf[0, PAD + a : PAD + b, :] = jnp.zeros((b - a, cols), jnp.float32)

    partners = [(dt, ds) for _, _, (dt, ds) in routes] + [(-dt, -ds) for _, _, (dt, ds) in routes]
    barrier = pltpu.get_barrier_semaphore()
    peers = 0
    for dt, ds in partners:
        @pl.when(inside(me_t + dt, me_s + ds))
        def _():
            pl.semaphore_signal(
                barrier, 1, device_id=(me_t + dt, me_s + ds), device_id_type=MESH
            )
        peers = peers + _present(me_t, dt, tms) * _present(me_s, ds, sps)
    pl.semaphore_wait(barrier, peers)

    copies = []
    for slot, ((a, b), (c, d), (dt, ds)) in enumerate(routes):
        incoming = pltpu.make_async_remote_copy(
            src_ref=outgoing.at[pl.ds(c, d - c)],
            dst_ref=buf.at[0, pl.ds(PAD + a, b - a)],
            send_sem=send_sems.at[slot],
            recv_sem=recv_sems.at[slot],
            device_id=(me_t - dt, me_s - ds),
            device_id_type=MESH,
        )

        @pl.when(inside(me_t - dt, me_s - ds))
        def _():
            incoming.wait_recv()

        copies.append(
            pltpu.make_async_remote_copy(
                src_ref=outgoing.at[pl.ds(c, d - c)],
                dst_ref=buf.at[0, pl.ds(PAD + a, b - a)],
                send_sem=send_sems.at[slot],
                recv_sem=recv_sems.at[slot],
                device_id=(me_t + dt, me_s + ds),
                device_id_type=MESH,
            )
        )

    prev_ref[...] = buf[0, PAD : PAD + span, :]
    for step in range(SUBSTEPS // 2):
        _stencil(buf, b_ref, first, span, cols, 0, 1, False)
        _stencil(buf, b_ref, first, span, cols, 1, 0, False)
    mine = buf[0, PAD + halo : PAD + halo + rows, :] + defect_ref[...]
    mine_ref[...] = mine
    outgoing[...] = mine
    for copy, (_, _, (dt, ds)) in zip(copies, routes):
        @pl.when(inside(me_t + dt, me_s + ds))
        def _():
            copy.start()
    for copy, (_, _, (dt, ds)) in zip(copies, routes):
        @pl.when(inside(me_t + dt, me_s + ds))
        def _():
            copy.wait_send()


def level_chain(defect, spread, halo, cid):
    rows, cols = defect.shape
    span = rows + 2 * halo
    kernel = functools.partial(_level_kernel, halo, COEFF_HALO - halo)
    return pl.pallas_call(
        kernel,
        out_shape=[
            jax.ShapeDtypeStruct((span, cols), jnp.float32),
            jax.ShapeDtypeStruct((rows, cols), jnp.float32),
        ],
        in_specs=[pl.BlockSpec(memory_space=pltpu.VMEM)] * 2,
        out_specs=[pl.BlockSpec(memory_space=pltpu.VMEM)] * 2,
        scratch_shapes=[
            pltpu.VMEM((2, span + 2 * PAD, cols), jnp.float32),
            pltpu.VMEM((rows, cols), jnp.float32),
            pltpu.SemaphoreType.DMA((3,)),
            pltpu.SemaphoreType.DMA((3,)),
        ],
        compiler_params=pltpu.CompilerParams(collective_id=cid, has_side_effects=True),
    )(defect, spread)


def moved(x, dt, ds):
    tms, sps = lax.axis_size("tm"), lax.axis_size("space")
    pairs = [
        (t * sps + s, (t + dt) * sps + (s + ds))
        for t in range(tms)
        for s in range(sps)
        if 0 <= t + dt < tms and 0 <= s + ds < sps
    ]
    return lax.ppermute(x, ("tm", "space"), pairs)


def with_halo(block, width, dt=0):
    rows = block.shape[-2]
    low = moved(block[..., rows - width :, :], dt, 1)
    high = moved(block[..., :width, :], dt, -1)
    middle = block if dt == 0 else moved(block, dt, 0)
    return jnp.concatenate([low, middle, high], axis=-2)


def trim(x, halo, keep):
    return x[..., halo - keep : x.shape[-2] - halo + keep, :]


def substep(extended, window, step_scale, with_source):
    middle = extended[..., 1:-1, :]
    north_row = extended[..., :-2, :]
    south_row = extended[..., 2:, :]
    widths = [(0, 0)] * (middle.ndim - 1) + [(1, 1)]
    padded = jnp.pad(middle, widths)
    west_col = padded[..., :-2]
    east_col = padded[..., 2:]
    rate_field = window[0]
    inflow = rate_field * (
        north_row
        + south_row
        + west_col
        + east_col
        + window[1] * (west_col - east_col)
        + window[2] * (north_row - south_row)
    )
    if with_source:
        inflow = inflow + window[3]
    return (middle + step_scale * inflow) / (1.0 + 4.0 * step_scale * rate_field)


def advance(fields, halo, count, coeffs, step_scale, with_source):
    inner = coeffs.shape[-2] - 2 * COEFF_HALO
    for position in range(count):
        out_halo = halo - position - 1
        first = COEFF_HALO - out_halo
        window = coeffs[:, first : first + inner + 2 * out_halo, :]
        fields = substep(fields, window, step_scale, with_source)
    return fields


def on_device(start_field, guessed, diffusion, peclet_x, peclet_y, source):
    rows, cols = start_field.shape
    R, H, L, h = rows, COEFF_HALO, LEVEL_HALO, SWEEP
    F = fixed_rows
    stacked = jnp.stack([diffusion, peclet_x, peclet_y, source], 0)
    first_points = [
        (0, (slice(0, 3), slice(0, R)), 0, F((slice(1, 4), slice(h, h + R))), None, False),
        (0, (slice(0, 3), slice(R - h, R)), 0, F((slice(1, 4), slice(0, h))), (0, 1), False),
        (0, (slice(0, 3), slice(0, h)), 0, F((slice(1, 4), slice(h + R, 2 * h + R))), (0, -1), False),
        (0, (3, slice(0, R)), 0, F((0, slice(h, h + R))), (1, 0), False),
        (0, (3, slice(R - h, R)), 0, F((0, slice(0, h))), (1, 1), False),
        (0, (3, slice(0, h)), 0, F((0, slice(h + R, 2 * h + R))), (1, -1), False),
        (1, (slice(0, R),), 1, F((slice(H, H + R),)), None, False),
        (1, (slice(R - H, R),), 1, F((slice(0, H),)), (0, 1), False),
        (1, (slice(0, H),), 1, F((slice(H + R, 2 * H + R),)), (0, -1), False),
        (2, (slice(0, 4), slice(0, R)), 2, F((slice(0, 4), slice(H, H + R))), None, False),
        (2, (slice(0, 4), slice(R - H, R)), 2, F((slice(0, 4), slice(0, H))), (0, 1), False),
        (2, (slice(0, 4), slice(0, H)), 2, F((slice(0, 4), slice(H + R, 2 * H + R))), (0, -1), False),
    ]
    ext1, start_ext, coeffs = exchange(
        [guessed, start_field, stacked],
        [(4, 2 * h + R, cols), (2 * H + R, cols), (4, 2 * H + R, cols)],
        first_points,
        1,
    )
    my_index = lax.axis_index("tm")
    first_slab = my_index == 0
    level_scale = float(COARSEN_ONE)
    top_scale = float(COARSEN_ONE * COARSEN_TWO)

    opening = jnp.where(first_slab, trim(start_ext, H, h), ext1[0])
    before1 = jnp.concatenate([opening[None], ext1[1:]], 0)
    fine = weights(coeffs, 1.0)
    settled = sweep(before1, h, SWEEP, fine, True)

    second_points = [
        (0, (slice(0, 4), slice(0, R)), 0, F((slice(1, 5), slice(H, H + R))), None, False),
        (0, (slice(0, 4), slice(R - H, R)), 0, F((slice(1, 5), slice(0, H))), (0, 1), False),
        (0, (slice(0, 4), slice(0, H)), 0, F((slice(1, 5), slice(H + R, 2 * H + R))), (0, -1), False),
        (0, (3, slice(0, R)), 0, F((0, slice(H, H + R))), (1, 0), False),
        (0, (3, slice(R - H, R)), 0, F((0, slice(0, H))), (1, 1), False),
        (0, (3, slice(0, H)), 0, F((0, slice(H + R, 2 * H + R))), (1, -1), False),
    ]
    (ext2,) = exchange([settled], [(5, 2 * H + R, cols)], second_points, 2)
    opening = jnp.where(first_slab, start_ext, ext2[0])
    before2 = jnp.concatenate([opening[None], ext2[1:4]], 0)
    swept = sweep(before2, H, SWEEP, fine, True)
    residual = swept - trim(ext2[1:5], H, H - SWEEP)
    stored = H - SWEEP

    def coarse(x, halo):
        return advance(x, halo, SUBSTEPS, coeffs, level_scale, False)

    def r_at(position, keep):
        return trim(residual[position], stored, keep)

    running = r_at(0, RES_HALO)
    halo = RES_HALO
    for position in range(1, COARSEN_TWO):
        running = coarse(running, halo) + r_at(position, halo - SUBSTEPS)
        halo -= SUBSTEPS
    c_value = running

    e = 4 * SUBSTEPS
    shift_points = [
        (0, (slice(0, R),), 0, F((slice(e, e + R),)), (1, 0), False),
        (0, (slice(R - e, R),), 0, F((slice(0, e),)), (1, 1), False),
        (0, (slice(0, e),), 0, F((slice(e + R, 2 * e + R),)), (1, -1), False),
    ]
    (entering,) = exchange([c_value], [(2 * e + R, cols)], shift_points, 3)
    running = entering
    halo = e
    for position in range(COARSEN_TWO - 1):
        running = coarse(running, halo) + r_at(position, halo - SUBSTEPS)
        halo -= SUBSTEPS
    defect = (r_at(COARSEN_TWO - 1, 0) + coarse(running, halo)) - c_value

    level_halo = 16
    prev_level, mine = level_chain(defect, weights(coeffs, top_scale), level_halo, 4)
    level_before = trim(prev_level, level_halo, RES_HALO)

    c_fixed = c_value + mine
    running = jnp.where(first_slab, 0.0, trim(entering, e, RES_HALO) + level_before)
    halo = RES_HALO
    pieces = []
    for position in range(COARSEN_TWO - 1):
        running = coarse(running, halo) + r_at(position, halo - SUBSTEPS)
        halo -= SUBSTEPS
        pieces.append(trim(running, halo, 0))
    pieces.append(c_fixed)
    return settled + jnp.stack(pieces, 0)


def solution(mesh):
    in_specs = (
        P("space", None),
        P("tm", "space", None),
        P("space", None),
        P("space", None),
        P("space", None),
        P("space", None),
    )
    out_specs = P("tm", "space", None)
    return jax.shard_map(
        on_device, mesh=mesh, in_specs=in_specs, out_specs=out_specs, check_vma=False
    )
```

```python
import functools

import jax
import jax.numpy as jnp
import numpy as np
from jax import lax
from jax.experimental import pallas as pl
from jax.experimental.pallas import tpu as pltpu
from jax.sharding import PartitionSpec as P

MESH = pl.DeviceIdType.MESH

SUBSTEPS = 4
COARSEN_ONE = 8
COARSEN_TWO = 4
SWEEP = SUBSTEPS * COARSEN_ONE
COEFF_HALO = 48
RES_HALO = 3 * SUBSTEPS
LEVEL_HALO = 40


def _shape_of(shape, index):
    return np.broadcast_to(np.float32(0), shape)[index].shape


def _present(index, offset, size):
    if offset >= 0:
        return 1 - (index + offset) // size
    return (index + offset + size) // size


def _exchange_kernel(n_in, n_out, entries, partners, fill_outs, zero_shape, *refs):
    ins = refs[:n_in]
    outs = refs[n_in : n_in + n_out]
    zeros, send_sems, recv_sems, local_sems, fill_sems, back_sems = refs[n_in + n_out :]
    me_t, me_s = lax.axis_index("tm"), lax.axis_index("space")
    tms, sps = lax.axis_size("tm"), lax.axis_size("space")

    def inside(t, s):
        return (t >= 0) & (t < tms) & (s >= 0) & (s < sps)

    def zero_view(shape):
        lead = (0,) * (3 - len(shape))
        return zeros.at[lead + tuple(slice(0, n) for n in shape)]

    zeros[...] = jnp.zeros_like(zeros)
    barrier = pltpu.get_barrier_semaphore()
    for dt, ds in partners:
        @pl.when(inside(me_t + dt, me_s + ds))
        def _():
            pl.semaphore_signal(
                barrier, 1, device_id=(me_t + dt, me_s + ds), device_id_type=MESH
            )
    peers = 0
    for dt, ds in partners:
        peers = peers + _present(me_t, dt, tms) * _present(me_s, ds, sps)
    pl.semaphore_wait(barrier, peers)

    remote = [e for e in entries if e[4] is not None]
    sends = []
    for slot, (src, src_index, dst, dst_index, offset, dynamic) in enumerate(remote):
        dt, ds = offset
        copy = pltpu.make_async_remote_copy(
            src_ref=ins[src].at[src_index],
            dst_ref=outs[dst].at[dst_index(me_t)],
            send_sem=send_sems.at[slot],
            recv_sem=recv_sems.at[slot],
            device_id=(me_t + dt, me_s + ds),
            device_id_type=MESH,
        )
        target = inside(me_t + dt, me_s + ds)

        @pl.when(target)
        def _():
            copy.start()

        sends.append((copy, target))

    locals_ = []
    for src, src_index, dst, dst_index, offset, dynamic in entries:
        if offset is not None:
            continue
        copy = pltpu.make_async_copy(
            ins[src].at[src_index], outs[dst].at[dst_index(me_t)], local_sems.at[len(locals_)]
        )
        copy.start()
        locals_.append(copy)

    fills = []
    for dst in fill_outs:
        for k in range(outs[dst].shape[0]):
            fill = pltpu.make_async_copy(
                zero_view(outs[dst].shape[1:]), outs[dst].at[k], fill_sems.at[len(fills)]
            )

            @pl.when(k > me_t)
            def _():
                fill.start()

            fills.append((k, fill))

    for slot, (src, src_index, dst, dst_index, offset, dynamic) in enumerate(remote):
        dt, ds = offset
        sender_t, sender_s = me_t - dt, me_s - ds
        has_sender = inside(sender_t, sender_s)
        incoming = pltpu.make_async_remote_copy(
            src_ref=ins[src].at[src_index],
            dst_ref=outs[dst].at[dst_index(sender_t)],
            send_sem=send_sems.at[slot],
            recv_sem=recv_sems.at[slot],
            device_id=(sender_t, sender_s),
            device_id_type=MESH,
        )

        @pl.when(has_sender)
        def _():
            incoming.wait_recv()

        missing = jnp.logical_not(has_sender)
        if dynamic:
            missing = missing & (sender_t >= 0) & (sender_t < tms)
        fallback = pltpu.make_async_copy(
            zero_view(_shape_of(ins[src].shape, src_index)),
            outs[dst].at[dst_index(sender_t)],
            back_sems.at[slot],
        )

        @pl.when(missing)
        def _():
            fallback.start()
            fallback.wait()

    for copy in locals_:
        copy.wait()
    for k, fill in fills:
        @pl.when(k > me_t)
        def _():
            fill.wait()
    for copy, target in sends:
        @pl.when(target)
        def _():
            copy.wait_send()


def exchange(inputs, out_shapes, entries, cid, fill_outs=()):
    partners = []
    for entry in entries:
        if entry[4] is None:
            continue
        dt, ds = entry[4]
        for o in ((dt, ds), (-dt, -ds)):
            if o not in partners:
                partners.append(o)
    shapes = [_shape_of(inputs[e[0]].shape, e[1]) for e in entries]
    shapes += [tuple(out_shapes[dst][1:]) for dst in fill_outs]
    padded = [(1,) * (3 - len(s)) + tuple(s) for s in shapes]
    zero_shape = tuple(max(s[i] for s in padded) for i in range(3))
    n_remote = sum(e[4] is not None for e in entries)
    n_local = sum(e[4] is None for e in entries)
    n_fill = sum(out_shapes[dst][0] for dst in fill_outs)
    kernel = functools.partial(
        _exchange_kernel,
        len(inputs),
        len(out_shapes),
        tuple(entries),
        tuple(partners),
        tuple(fill_outs),
        zero_shape,
    )
    return pl.pallas_call(
        kernel,
        out_shape=[jax.ShapeDtypeStruct(s, jnp.float32) for s in out_shapes],
        in_specs=[pl.BlockSpec(memory_space=pltpu.VMEM)] * len(inputs),
        out_specs=[pl.BlockSpec(memory_space=pl.ANY)] * len(out_shapes),
        scratch_shapes=[
            pltpu.VMEM(zero_shape, jnp.float32),
            pltpu.SemaphoreType.DMA((max(n_remote, 1),)),
            pltpu.SemaphoreType.DMA((max(n_remote, 1),)),
            pltpu.SemaphoreType.DMA((max(n_local, 1),)),
            pltpu.SemaphoreType.DMA((max(n_fill, 1),)),
            pltpu.SemaphoreType.DMA((max(n_remote, 1),)),
        ],
        compiler_params=pltpu.CompilerParams(collective_id=cid, has_side_effects=True),
    )(*inputs)


def fixed_rows(index):
    return lambda sender: index


CHUNK = 8
PAD = 8


def _stencil(buf, b_ref, first, rows, cols, src, dst, with_source):
    for c0 in range(0, rows, CHUNK):
        def weight(k):
            return b_ref[k, pl.ds(first + c0, CHUNK), :]

        centre = buf[src, pl.ds(PAD + c0, CHUNK), :]
        north_row = buf[src, pl.ds(PAD + c0 - 1, CHUNK), :]
        south_row = buf[src, pl.ds(PAD + c0 + 1, CHUNK), :]
        west_col = pltpu.roll(centre, 1, 1)
        east_col = pltpu.roll(centre, cols - 1, 1)
        new = (
            weight(0) * centre
            + weight(1) * north_row
            + weight(2) * south_row
            + weight(3) * west_col
            + weight(4) * east_col
        )
        if with_source:
            new = new + weight(5)
        buf[dst, pl.ds(PAD + c0, CHUNK), :] = new


def _sweep_kernel(count, with_source, first, x_ref, b_ref, o_ref, buf):
    fields, rows, cols = x_ref.shape
    buf[:, 0:PAD, :] = jnp.zeros((2, PAD, cols), jnp.float32)
    buf[:, PAD + rows : 2 * PAD + rows, :] = jnp.zeros((2, PAD, cols), jnp.float32)

    def two(step, carry):
        _stencil(buf, b_ref, first, rows, cols, 0, 1, with_source)
        _stencil(buf, b_ref, first, rows, cols, 1, 0, with_source)
        return carry

    for f in range(fields):
        buf[0, PAD : PAD + rows, :] = x_ref[f]
        lax.fori_loop(0, count // 2, two, 0, unroll=4)
        o_ref[f] = buf[0, pl.ds(PAD + count, rows - 2 * count), :]


def weights(coeffs, step_scale):
    diffusion, peclet_x, peclet_y, source = coeffs
    share = 1.0 / (1.0 + 4.0 * step_scale * diffusion)
    rate = step_scale * diffusion * share
    column = lax.broadcasted_iota(jnp.int32, diffusion.shape, diffusion.ndim - 1)
    cols = diffusion.shape[-1]
    return jnp.stack(
        [
            share,
            rate * (1.0 + peclet_y),
            rate * (1.0 - peclet_y),
            jnp.where(column == 0, 0.0, rate * (1.0 + peclet_x)),
            jnp.where(column == cols - 1, 0.0, rate * (1.0 - peclet_x)),
            step_scale * source * share,
        ],
        0,
    )


def sweep(fields, halo, count, spread, with_source):
    n, rows, cols = fields.shape
    kernel = functools.partial(_sweep_kernel, count, with_source, COEFF_HALO - halo)
    return pl.pallas_call(
        kernel,
        out_shape=jax.ShapeDtypeStruct((n, rows - 2 * count, cols), jnp.float32),
        in_specs=[pl.BlockSpec(memory_space=pltpu.VMEM)] * 2,
        out_specs=pl.BlockSpec(memory_space=pltpu.VMEM),
        scratch_shapes=[pltpu.VMEM((2, rows + 2 * PAD, cols), jnp.float32)],
        cost_estimate=pl.CostEstimate(
            flops=12 * n * rows * cols * count, transcendentals=0, bytes_accessed=4 * (n + 6) * rows * cols
        ),
    )(fields, spread)


def _level_kernel(halo, first, defect_ref, b_ref, prev_ref, mine_ref, buf, outgoing, send_sems, recv_sems):
    rows, cols = defect_ref.shape
    span = rows + 2 * halo
    me_t, me_s = lax.axis_index("tm"), lax.axis_index("space")
    tms, sps = lax.axis_size("tm"), lax.axis_size("space")

    def inside(t, s):
        return (t >= 0) & (t < tms) & (s >= 0) & (s < sps)

    buf[:, 0:PAD, :] = jnp.zeros((2, PAD, cols), jnp.float32)
    buf[:, PAD + span : 2 * PAD + span, :] = jnp.zeros((2, PAD, cols), jnp.float32)
    routes = (
        ((halo, halo + rows), (0, rows), (1, 0)),
        ((0, halo), (rows - halo, rows), (1, 1)),
        ((halo + rows, span), (0, halo), (1, -1)),
    )
    for (a, b), _, (dt, ds) in routes:
        @pl.when(jnp.logical_not(inside(me_t - dt, me_s - ds)))
        def _():
            buf[0, PAD + a : PAD + b, :] = jnp.zeros((b - a, cols), jnp.float32)

    partners = [(dt, ds) for _, _, (dt, ds) in routes] + [(-dt, -ds) for _, _, (dt, ds) in routes]
    barrier = pltpu.get_barrier_semaphore()
    peers = 0
    for dt, ds in partners:
        @pl.when(inside(me_t + dt, me_s + ds))
        def _():
            pl.semaphore_signal(
                barrier, 1, device_id=(me_t + dt, me_s + ds), device_id_type=MESH
            )
        peers = peers + _present(me_t, dt, tms) * _present(me_s, ds, sps)
    pl.semaphore_wait(barrier, peers)

    copies = []
    for slot, ((a, b), (c, d), (dt, ds)) in enumerate(routes):
        incoming = pltpu.make_async_remote_copy(
            src_ref=outgoing.at[pl.ds(c, d - c)],
            dst_ref=buf.at[0, pl.ds(PAD + a, b - a)],
            send_sem=send_sems.at[slot],
            recv_sem=recv_sems.at[slot],
            device_id=(me_t - dt, me_s - ds),
            device_id_type=MESH,
        )

        @pl.when(inside(me_t - dt, me_s - ds))
        def _():
            incoming.wait_recv()

        copies.append(
            pltpu.make_async_remote_copy(
                src_ref=outgoing.at[pl.ds(c, d - c)],
                dst_ref=buf.at[0, pl.ds(PAD + a, b - a)],
                send_sem=send_sems.at[slot],
                recv_sem=recv_sems.at[slot],
                device_id=(me_t + dt, me_s + ds),
                device_id_type=MESH,
            )
        )

    prev_ref[...] = buf[0, PAD : PAD + span, :]
    for step in range(SUBSTEPS // 2):
        _stencil(buf, b_ref, first, span, cols, 0, 1, False)
        _stencil(buf, b_ref, first, span, cols, 1, 0, False)
    mine = buf[0, PAD + halo : PAD + halo + rows, :] + defect_ref[...]
    mine_ref[...] = mine
    outgoing[...] = mine
    for copy, (_, _, (dt, ds)) in zip(copies, routes):
        @pl.when(inside(me_t + dt, me_s + ds))
        def _():
            copy.start()
    for copy, (_, _, (dt, ds)) in zip(copies, routes):
        @pl.when(inside(me_t + dt, me_s + ds))
        def _():
            copy.wait_send()


def level_chain(defect, spread, halo, cid):
    rows, cols = defect.shape
    span = rows + 2 * halo
    kernel = functools.partial(_level_kernel, halo, COEFF_HALO - halo)
    return pl.pallas_call(
        kernel,
        out_shape=[
            jax.ShapeDtypeStruct((span, cols), jnp.float32),
            jax.ShapeDtypeStruct((rows, cols), jnp.float32),
        ],
        in_specs=[pl.BlockSpec(memory_space=pltpu.VMEM)] * 2,
        out_specs=[pl.BlockSpec(memory_space=pltpu.VMEM)] * 2,
        scratch_shapes=[
            pltpu.VMEM((2, span + 2 * PAD, cols), jnp.float32),
            pltpu.VMEM((rows, cols), jnp.float32),
            pltpu.SemaphoreType.DMA((3,)),
            pltpu.SemaphoreType.DMA((3,)),
        ],
        compiler_params=pltpu.CompilerParams(collective_id=cid, has_side_effects=True),
    )(defect, spread)


def moved(x, dt, ds):
    tms, sps = lax.axis_size("tm"), lax.axis_size("space")
    pairs = [
        (t * sps + s, (t + dt) * sps + (s + ds))
        for t in range(tms)
        for s in range(sps)
        if 0 <= t + dt < tms and 0 <= s + ds < sps
    ]
    return lax.ppermute(x, ("tm", "space"), pairs)


def with_halo(block, width, dt=0):
    rows = block.shape[-2]
    low = moved(block[..., rows - width :, :], dt, 1)
    high = moved(block[..., :width, :], dt, -1)
    middle = block if dt == 0 else moved(block, dt, 0)
    return jnp.concatenate([low, middle, high], axis=-2)


def trim(x, halo, keep):
    return x[..., halo - keep : x.shape[-2] - halo + keep, :]


def substep(extended, window, step_scale, with_source):
    middle = extended[..., 1:-1, :]
    north_row = extended[..., :-2, :]
    south_row = extended[..., 2:, :]
    widths = [(0, 0)] * (middle.ndim - 1) + [(1, 1)]
    padded = jnp.pad(middle, widths)
    west_col = padded[..., :-2]
    east_col = padded[..., 2:]
    rate_field = window[0]
    inflow = rate_field * (
        north_row
        + south_row
        + west_col
        + east_col
        + window[1] * (west_col - east_col)
        + window[2] * (north_row - south_row)
    )
    if with_source:
        inflow = inflow + window[3]
    return (middle + step_scale * inflow) / (1.0 + 4.0 * step_scale * rate_field)


def advance(fields, halo, count, coeffs, step_scale, with_source):
    inner = coeffs.shape[-2] - 2 * COEFF_HALO
    for position in range(count):
        out_halo = halo - position - 1
        first = COEFF_HALO - out_halo
        window = coeffs[:, first : first + inner + 2 * out_halo, :]
        fields = substep(fields, window, step_scale, with_source)
    return fields


def on_device(start_field, guessed, diffusion, peclet_x, peclet_y, source):
    rows, cols = start_field.shape
    R, H, L, h = rows, COEFF_HALO, LEVEL_HALO, SWEEP
    F = fixed_rows
    stacked = jnp.stack([diffusion, peclet_x, peclet_y, source], 0)
    first_points = [
        (0, (slice(0, 3), slice(0, R)), 0, F((slice(1, 4), slice(h, h + R))), None, False),
        (0, (slice(0, 3), slice(R - h, R)), 0, F((slice(1, 4), slice(0, h))), (0, 1), False),
        (0, (slice(0, 3), slice(0, h)), 0, F((slice(1, 4), slice(h + R, 2 * h + R))), (0, -1), False),
        (0, (3, slice(0, R)), 0, F((0, slice(h, h + R))), (1, 0), False),
        (0, (3, slice(R - h, R)), 0, F((0, slice(0, h))), (1, 1), False),
        (0, (3, slice(0, h)), 0, F((0, slice(h + R, 2 * h + R))), (1, -1), False),
        (1, (slice(0, R),), 1, F((slice(H, H + R),)), None, False),
        (1, (slice(R - H, R),), 1, F((slice(0, H),)), (0, 1), False),
        (1, (slice(0, H),), 1, F((slice(H + R, 2 * H + R),)), (0, -1), False),
        (2, (slice(0, 4), slice(0, R)), 2, F((slice(0, 4), slice(H, H + R))), None, False),
        (2, (slice(0, 4), slice(R - H, R)), 2, F((slice(0, 4), slice(0, H))), (0, 1), False),
        (2, (slice(0, 4), slice(0, H)), 2, F((slice(0, 4), slice(H + R, 2 * H + R))), (0, -1), False),
    ]
    ext1, start_ext, coeffs = exchange(
        [guessed, start_field, stacked],
        [(4, 2 * h + R, cols), (2 * H + R, cols), (4, 2 * H + R, cols)],
        first_points,
        1,
    )
    my_index = lax.axis_index("tm")
    first_slab = my_index == 0
    level_scale = float(COARSEN_ONE)
    top_scale = float(COARSEN_ONE * COARSEN_TWO)

    opening = jnp.where(first_slab, trim(start_ext, H, h), ext1[0])
    before1 = jnp.concatenate([opening[None], ext1[1:]], 0)
    fine = weights(coeffs, 1.0)
    settled = sweep(before1, h, SWEEP, fine, True)

    second_points = [
        (0, (slice(0, 4), slice(0, R)), 0, F((slice(1, 5), slice(H, H + R))), None, False),
        (0, (slice(0, 4), slice(R - H, R)), 0, F((slice(1, 5), slice(0, H))), (0, 1), False),
        (0, (slice(0, 4), slice(0, H)), 0, F((slice(1, 5), slice(H + R, 2 * H + R))), (0, -1), False),
        (0, (3, slice(0, R)), 0, F((0, slice(H, H + R))), (1, 0), False),
        (0, (3, slice(R - H, R)), 0, F((0, slice(0, H))), (1, 1), False),
        (0, (3, slice(0, H)), 0, F((0, slice(H + R, 2 * H + R))), (1, -1), False),
    ]
    (ext2,) = exchange([settled], [(5, 2 * H + R, cols)], second_points, 2)
    opening = jnp.where(first_slab, start_ext, ext2[0])
    before2 = jnp.concatenate([opening[None], ext2[1:4]], 0)
    swept = sweep(before2, H, SWEEP, fine, True)
    residual = swept - trim(ext2[1:5], H, H - SWEEP)
    stored = H - SWEEP

    def coarse(x, halo):
        return advance(x, halo, SUBSTEPS, coeffs, level_scale, False)

    def r_at(position, keep):
        return trim(residual[position], stored, keep)

    running = r_at(0, RES_HALO)
    halo = RES_HALO
    for position in range(1, COARSEN_TWO):
        running = coarse(running, halo) + r_at(position, halo - SUBSTEPS)
        halo -= SUBSTEPS
    c_value = running

    e = 4 * SUBSTEPS
    shift_points = [
        (0, (slice(0, R),), 0, F((slice(e, e + R),)), (1, 0), False),
        (0, (slice(R - e, R),), 0, F((slice(0, e),)), (1, 1), False),
        (0, (slice(0, e),), 0, F((slice(e + R, 2 * e + R),)), (1, -1), False),
    ]
    (entering,) = exchange([c_value], [(2 * e + R, cols)], shift_points, 3)
    running = entering
    halo = e
    for position in range(COARSEN_TWO - 1):
        running = coarse(running, halo) + r_at(position, halo - SUBSTEPS)
        halo -= SUBSTEPS
    defect = (r_at(COARSEN_TWO - 1, 0) + coarse(running, halo)) - c_value

    level_halo = 16
    prev_level, mine = level_chain(defect, weights(coeffs, top_scale), level_halo, 4)
    level_before = trim(prev_level, level_halo, RES_HALO)

    c_fixed = c_value + mine
    running = jnp.where(first_slab, 0.0, trim(entering, e, RES_HALO) + level_before)
    halo = RES_HALO
    pieces = []
    for position in range(COARSEN_TWO - 1):
        running = coarse(running, halo) + r_at(position, halo - SUBSTEPS)
        halo -= SUBSTEPS
        pieces.append(trim(running, halo, 0))
    pieces.append(c_fixed)
    return settled + jnp.stack(pieces, 0)


def solution(mesh):
    in_specs = (
        P("space", None),
        P("tm", "space", None),
        P("space", None),
        P("space", None),
        P("space", None),
        P("space", None),
    )
    out_specs = P("tm", "space", None)
    return jax.shard_map(
        on_device, mesh=mesh, in_specs=in_specs, out_specs=out_specs, check_vma=False
    )
```
